32 devices in a mesh: groups: 2 (over y), tile: 4 (over z), col: 2 (over x), rep: 2 (over core).
Axes of the slice: x: 2, y: 2, z: 4, core: 2. Of those that a mesh axis runs over, the one named last changes fastest.
Arguments:
- forcing: bfloat16 [4, 20, 32, 2048], P(('groups', 'rep'), 'tile', None, 'col'), parts along dimension 0, may hold values from -6 to 6
- member_kernel_weight: bfloat16 [20, 576, 64], P('tile'), may hold values from -0.25 to 0.25
- member_counts: int32 [4], P('tile'), may hold values from 1 to 5, 16 in all
- mixing_input_weight: bfloat16 [1280, 512], P('tile'), may hold values from -0.1875 to 0.1875
- depth_weight: float32 [9, 512], replicated, may hold values from -2 to 2
- mix_weight: bfloat16 [512, 512], replicated, may hold values from -0.25 to 0.25
- cotangent: bfloat16 [4, 32, 32, 512], P(('groups', 'rep'), 'tile', 'col'), parts along dimension 0, may hold values from -6 to 6
Outputs:
- adjusted: bfloat16 [4, 32, 32, 512], P(('groups', 'rep'), 'tile', 'col'), parts along dimension 0
- mix_grad: float32 [1024, 512], P(('groups', 'tile', 'col', 'rep')), parts along dimension 0
- depth_grad: float32 [18, 512], P('groups'), parts along dimension 0
- in_grad: float32 [2560, 512], P(('groups', 'tile')), parts along dimension 0
- group_grad: float32 [40, 576, 64], P(('groups', 'tile')), parts along dimension 0
The draws below stay inside these ranges and needn't reach their ends.
There are 2 independent parts, one for each index of `groups`. The reference program is written for one: setup_inputs(seed, part) draws one part's arguments, and reference() takes and returns one part's arrays. A program takes and returns all parts, laid end to end along the dimension named above; an argument that names none is the same for every part. Nothing has to cross between parts.
Inputs may be any that keep to these rules, and one draw needn't show every extreme that they name: member_counts sums to 16; each index of tile holds at least one member and at least one holds 5.
All inputs are finite; a program needn't handle non-finite values. No bound on the sum of `member_counts` on one device may be relied on, other than what follows from the above.
Results may differ from the reference program's by a relative error of at most 0.011.
Values may be sent and summed in bfloat16 or wider, within the bound.
No kernel may reach another device: no remote copies, remote signals or barrier semaphores. Data moves between devices by JAX's collectives and lax.ppermute only.
A program may use at most 64 MiB of HBM per device.

```python
import math
import jax
import jax.numpy as jnp
import numpy as np
from jax import lax

MEMBER_CHANNELS = 64
MIXING_CHANNELS = 512
SLOTS = 5
SLOT_TOTAL = 20
HELD_MEMBERS = 16
GRID_ROWS = 32
GRID_COLUMNS = 32
BATCH_SAMPLES = 2
N_TILE = 4


def strengthened(result, key, source, target, parts, factor):
    def block_of(dim):
        return (jnp.arange(result.shape[dim]) // (result.shape[dim] // parts)).reshape((-1,) + (1,) * (result.ndim - 1 - dim))

    one_side = jax.random.permutation(key, parts)[block_of(target)]
    other_side = (block_of(target) + parts // 2) % parts
    return jnp.where((block_of(source) == one_side) | (block_of(source) == other_side), factor * result, result)


def shard_levels(rng, shape, cuts, least, high):
    def one(dim, parts):
        draws = jax.random.uniform(jax.random.fold_in(jax.random.fold_in(rng, 6), dim), (parts,), jnp.float32, least / len(cuts), high / len(cuts))
        return jnp.repeat(jnp.exp(draws), shape[dim] // parts).reshape((-1,) + (1,) * (len(shape) - dim - 1))

    level = one(*cuts[0])
    for cut in cuts[1:]:
        level = level * one(*cut)
    return level


def length_profile(number_of, total, most, lean):
    loads = [(1 << 20) // math.isqrt(rank ** lean) + 1 for rank in range(2, number_of + 1)]
    rest, holding = total - most - (number_of - 1), [1] * (number_of - 1)
    while rest > 0:
        free = [i for i in range(number_of - 1) if holding[i] < most]
        pool, remaining = sum([loads[i] for i in free]), rest
        for i in free:
            more = min(most - holding[i], max(1, remaining * loads[i] // pool), rest)
            holding[i] = holding[i] + more
            rest = rest - more
    return np.array([most] + holding)


def uneven_parts(rng, count, total, limit, slope):
    if count == 2:
        one = jax.random.randint(rng, (), max(1, total - limit), min(limit, total - 1) + 1)
        return jnp.stack([one, total - one])
    sizes = jnp.asarray(length_profile(count, total, limit, slope), jnp.int32)
    twos = (count - 1) // 2
    donor, receiver = sizes[1:1 + 2 * twos:2], sizes[2:2 + 2 * twos:2]
    slack = jnp.minimum(donor - 1, limit - receiver)
    moved = jax.random.randint(jax.random.fold_in(rng, 1), (twos,), 0, 1 << 20) % (slack + 1)
    sizes = sizes.at[1:1 + 2 * twos:2].set(donor - moved).at[2:2 + 2 * twos:2].set(receiver + moved)
    return sizes[jax.random.permutation(jax.random.fold_in(rng, 2), count)]


def scatter_about(key, shape, scale, most, pieces=(), kind=jnp.bfloat16):
    loudness = shard_levels(key, shape, pieces, -0.22, 0.18) if pieces else 1.0
    array = jax.random.normal(key, shape, jnp.float32) * scale * loudness
    return jnp.minimum(jnp.maximum(array, -most), most).astype(kind)


def gaussian_with(rng, extent, spread, limit, cuts, heavy, dtype=jnp.bfloat16):
    entries = spread * jax.random.normal(rng, extent, jnp.float32)
    if cuts:
        entries = entries * shard_levels(rng, extent, cuts, -0.22, 0.18)
    return jnp.clip(strengthened(entries, jax.random.fold_in(rng, 3), *heavy), -limit, limit).astype(dtype)


def setup_inputs(seed: int = 0, part: int = 0) -> dict:
    key_list = jax.random.split(jax.random.key(seed), 8)
    part_keys = jax.random.split(jax.random.fold_in(key_list[7], part), 8)
    return {
        "forcing": scatter_about(part_keys[0], (BATCH_SAMPLES, SLOT_TOTAL, GRID_ROWS, GRID_COLUMNS * MEMBER_CHANNELS), 1.0, 6.0, ((0, 2), (1, 4), (3, 2))),
        "member_kernel_weight": scatter_about(key_list[1], (SLOT_TOTAL, 9 * MEMBER_CHANNELS, MEMBER_CHANNELS), (9 * MEMBER_CHANNELS) ** -0.5, 0.25, ((0, 4),)),
        "member_counts": uneven_parts(key_list[2], N_TILE, HELD_MEMBERS, SLOTS, 2).astype(jnp.int32),
        "mixing_input_weight": scatter_about(key_list[3], (SLOT_TOTAL * MEMBER_CHANNELS, MIXING_CHANNELS), (HELD_MEMBERS * MEMBER_CHANNELS) ** -0.5, 0.1875, ((0, 4),)),
        "depth_weight": scatter_about(key_list[4], (9, MIXING_CHANNELS), 9 ** -0.5, 2.0, (), jnp.float32),
        "mix_weight": scatter_about(key_list[5], (MIXING_CHANNELS, MIXING_CHANNELS), MIXING_CHANNELS ** -0.5, 0.25),
        "cotangent": gaussian_with(part_keys[6], (BATCH_SAMPLES, GRID_ROWS, GRID_COLUMNS, MIXING_CHANNELS), 1.0, 6.0, ((0, 2), (1, 4), (2, 2)), (1, 3, 4, 2.0)),
    }


def silu_slope(value):
    sig = jax.nn.sigmoid(value)
    return sig * (1.0 + value * (1.0 - sig))


def patches(field):
    height, width = field.shape[0], field.shape[1]
    padded = jnp.pad(field, ((1, 1), (1, 1), (0, 0)))
    return jnp.concatenate([padded[down:down + height, across:across + width] for down in range(3) for across in range(3)], axis=-1)


def reference(forcing, member_kernel_weight, member_counts, mixing_input_weight, depth_weight, mix_weight, cotangent):
    member_slot_index = jnp.arange(SLOT_TOTAL).astype(jnp.int32)
    live = (member_slot_index % SLOTS < member_counts[member_slot_index // SLOTS]).astype(jnp.float32)
    input_images = jnp.transpose(forcing, (1, 0, 2, 3)).reshape(SLOT_TOTAL, BATCH_SAMPLES, GRID_ROWS, GRID_COLUMNS, MEMBER_CHANNELS)

    def forward_slot(packed):
        image, weight, alive = packed
        columns = jax.vmap(patches)(image).reshape(-1, 9 * MEMBER_CHANNELS)
        gate = jnp.dot(columns, weight, preferred_element_type=jnp.float32)
        return (jax.nn.silu(gate) * alive).astype(jnp.bfloat16).reshape(BATCH_SAMPLES, GRID_ROWS, GRID_COLUMNS, MEMBER_CHANNELS)

    feature_maps = lax.map(forward_slot, (input_images, member_kernel_weight, live))
    feature_maps = jnp.transpose(feature_maps, (1, 2, 3, 0, 4)).reshape(-1, SLOT_TOTAL * MEMBER_CHANNELS)
    mixed_in = jnp.dot(feature_maps, mixing_input_weight, preferred_element_type=jnp.float32).astype(jnp.bfloat16)
    mixed_in = mixed_in.reshape(BATCH_SAMPLES, GRID_ROWS, GRID_COLUMNS, MIXING_CHANNELS)
    act_pad = jnp.pad(mixed_in, ((0, 0), (1, 1), (1, 1), (0, 0))).astype(jnp.float32)
    before = jnp.zeros((BATCH_SAMPLES, GRID_ROWS, GRID_COLUMNS, MIXING_CHANNELS), jnp.float32)
    for down in range(3):
        for across in range(3):
            before = before + depth_weight[down * 3 + across] * act_pad[:, down:down + GRID_ROWS, across:across + GRID_COLUMNS]
    hidden = jax.nn.silu(before).astype(jnp.bfloat16)
    flat_hidden = hidden.reshape(-1, MIXING_CHANNELS)
    adjusted = jnp.dot(flat_hidden, mix_weight.T, preferred_element_type=jnp.float32).astype(jnp.bfloat16)
    adjusted = adjusted.reshape(BATCH_SAMPLES, GRID_ROWS, GRID_COLUMNS, MIXING_CHANNELS)
    upstream = cotangent.reshape(-1, MIXING_CHANNELS)
    hidden_grad = jnp.dot(upstream, mix_weight, preferred_element_type=jnp.float32).reshape(BATCH_SAMPLES, GRID_ROWS, GRID_COLUMNS, MIXING_CHANNELS)
    before_grad = (hidden_grad * silu_slope(before)).astype(jnp.bfloat16)
    mix_grad = jnp.dot(upstream.T, flat_hidden, preferred_element_type=jnp.float32)
    grad_wide = before_grad.astype(jnp.float32)
    grad_pad = jnp.pad(grad_wide, ((0, 0), (1, 1), (1, 1), (0, 0)))
    depth_rows = []
    act_grad = jnp.zeros((BATCH_SAMPLES, GRID_ROWS, GRID_COLUMNS, MIXING_CHANNELS), jnp.float32)
    for down in range(3):
        for across in range(3):
            depth_rows.append(jnp.sum(act_pad[:, down:down + GRID_ROWS, across:across + GRID_COLUMNS] * grad_wide, axis=(0, 1, 2)))
            act_grad = act_grad + depth_weight[down * 3 + across] * grad_pad[:, 2 - down:2 - down + GRID_ROWS, 2 - across:2 - across + GRID_COLUMNS]
    depth_grad = jnp.stack(depth_rows, axis=0)
    flat_act_grad = act_grad.astype(jnp.bfloat16).reshape(-1, MIXING_CHANNELS)
    in_grad = jnp.dot(feature_maps.T, flat_act_grad, preferred_element_type=jnp.float32)
    feature_gradient = jnp.dot(flat_act_grad, mixing_input_weight.T, preferred_element_type=jnp.float32).astype(jnp.bfloat16)
    feature_gradient = jnp.transpose(feature_gradient.reshape(BATCH_SAMPLES, GRID_ROWS, GRID_COLUMNS, SLOT_TOTAL, MEMBER_CHANNELS), (3, 0, 1, 2, 4))

    def backward_slot(packed):
        image, weight, alive, slot_grad = packed
        columns = jax.vmap(patches)(image).reshape(-1, 9 * MEMBER_CHANNELS)
        gate = jnp.dot(columns, weight, preferred_element_type=jnp.float32)
        inner = (slot_grad.reshape(-1, MEMBER_CHANNELS).astype(jnp.float32) * silu_slope(gate) * alive).astype(jnp.bfloat16)
        return jnp.dot(columns.T, inner, preferred_element_type=jnp.float32)

    group_grad = lax.map(backward_slot, (input_images, member_kernel_weight, live, feature_gradient))
    return adjusted, mix_grad, depth_grad, in_grad, group_grad
```

```python
import jax
import jax.numpy as jnp
from jax import lax
from jax.sharding import PartitionSpec as P

F32 = jnp.float32
BF16 = jnp.bfloat16


def swap(value, axis, step):
    return lax.ppermute(value, axis, [(i, i ^ step) for i in range(lax.axis_size(axis))])


def edges(low, high, axis):
    count = lax.axis_size(axis)
    even = lax.axis_index(axis) % 2 == 0

    def exchange(value, first):
        pairs = [(i, i + 1) for i in range(first, count - 1, 2)]
        if not pairs:
            return jnp.zeros_like(value)
        return lax.ppermute(value, axis, pairs + [(b, a) for a, b in pairs])

    near = exchange(jnp.where(even, high, low), 0)
    far = exchange(jnp.where(even, low, high), 1)
    return jnp.where(even, far, near), jnp.where(even, near, far)


def tree_sum(terms):
    while len(terms) > 1:
        terms = [a + b for a, b in zip(terms[::2], terms[1::2])]
    return terms[0]


def scatter_sum(parts, extra, axis):
    mine = lax.axis_index(axis)
    size = parts.shape[1:]
    totals, extras = [lax.dynamic_index_in_dim(parts, mine, 0, False)], [extra.astype(BF16).astype(F32)]
    for step in range(1, lax.axis_size(axis)):
        part = lax.dynamic_index_in_dim(parts, mine ^ step, 0, False)
        flat = jnp.concatenate([part.reshape(-1, size[-1]), extra], axis=0).astype(BF16)
        flat = swap(flat, axis, step).astype(F32)
        rows = flat.shape[0] - extra.shape[0]
        totals.append(flat[:rows].reshape(size))
        extras.append(flat[rows:])
    return tree_sum(totals), tree_sum(extras)


def full_sum(term):
    mine = lax.axis_index("rep")
    half = term.shape[0] // 2
    parts = term.reshape((2, half) + term.shape[1:])
    own = lax.dynamic_index_in_dim(parts, mine, 0, False)
    other = lax.dynamic_index_in_dim(parts, 1 - mine, 0, False).astype(BF16)
    total = (own + swap(other, "rep", 1).astype(F32)).astype(BF16)
    step = 1
    while step < lax.axis_size("col"):
        total = (total.astype(F32) + swap(total, "col", step).astype(F32)).astype(BF16)
        step *= 2
    remote = swap(total, "rep", 1)
    first = mine == 0
    return jnp.concatenate([jnp.where(first, total, remote), jnp.where(first, remote, total)], axis=0)


def gathered_weight(weight):
    rows, hidden = weight.shape
    col, rep = lax.axis_index("col") % 2, lax.axis_index("rep")
    chunk = lax.dynamic_slice_in_dim(weight, (col * 2 + rep) * (rows // 4), rows // 4, axis=0)
    blocks = chunk[None]
    step = 1
    while step < lax.axis_size("tile"):
        blocks = jnp.concatenate([blocks, swap(blocks, "tile", step)], axis=0)
        step *= 2
    other = swap(blocks, "col", 1)
    pair = jnp.stack([jnp.where(col == 0, blocks, other), jnp.where(col == 0, other, blocks)], axis=1)
    other = swap(pair, "rep", 1)
    quad = jnp.stack([jnp.where(rep == 0, pair, other), jnp.where(rep == 0, other, pair)], axis=2)
    return quad.reshape(-1, rows, hidden)


def silu_slope(value):
    sig = jax.nn.sigmoid(value)
    return sig * (1.0 + value * (1.0 - sig))


def local(
    forcing,
    member_kernel_weight,
    member_counts,
    mixing_input_weight,
    depth_weight,
    mix_weight,
    cotangent,
):
    channels = member_kernel_weight.shape[2]
    slots = forcing.shape[1]
    height = forcing.shape[2]
    width = forcing.shape[3] // channels
    hidden = mixing_input_weight.shape[1]
    tiles, cols, reps = (lax.axis_size(a) for a in ("tile", "col", "rep"))
    tile, col = lax.axis_index("tile"), lax.axis_index("col")
    band = height // tiles

    field = forcing[0]
    reach = 3 * channels
    left, right = edges(field[..., :reach], field[..., -reach:], "col")
    weight_blocks = gathered_weight(mixing_input_weight)

    upstream = cotangent[0]
    low, high = edges(upstream[:, :1], upstream[:, -1:], "col")
    wide = jnp.concatenate([low, upstream, high], axis=1)
    low, high = edges(wide[:1], wide[-1:], "tile")
    wide = jnp.concatenate([low, wide, high], axis=0)
    hidden_grad = jnp.dot(wide.reshape(-1, hidden), mix_weight, preferred_element_type=F32)
    hidden_grad = hidden_grad.reshape(band + 2, width + 2, hidden)

    extended = jnp.concatenate([left, field, right], axis=-1).reshape(slots, height, width + 6, channels)
    padded = jnp.pad(extended, ((0, 0), (1, 1), (0, 0), (0, 0)))
    columns = jnp.concatenate(
        [padded[:, a : a + height, b : b + width + 4] for a in range(3) for b in range(3)], axis=-1
    )
    gate = jnp.einsum("krcp,kpd->krcd", columns, member_kernel_weight, preferred_element_type=F32)
    live = (jnp.arange(slots) < member_counts[0])[:, None, None, None]
    place = col * width + jnp.arange(width + 4) - 2
    inside = (place >= 0) & (place < width * cols)
    features = jnp.where(live & inside[:, None], jax.nn.silu(gate), 0.0).astype(BF16)
    features = jnp.transpose(features, (1, 2, 0, 3)).reshape(height, width + 4, slots * channels)
    own_features = features[:, 2:-2].reshape(-1, slots * channels)
    features = jnp.pad(features, ((2, 2), (0, 0), (0, 0)))

    pieces = []
    for step in range(tiles):
        piece = lax.dynamic_slice_in_dim(features, (tile ^ step) * band, band + 4, axis=0)
        piece = piece.reshape(-1, slots * channels)
        pieces.append(swap(piece, "tile", step) if step else piece)
    mixed = tree_sum(
        [jnp.dot(f, weight_blocks[k], preferred_element_type=F32) for k, f in enumerate(pieces)]
    )
    mixed = mixed.astype(BF16).astype(F32).reshape(band + 4, width + 4, hidden)

    before = 0.0
    for a in range(3):
        for b in range(3):
            before = before + depth_weight[a * 3 + b] * mixed[a : a + band + 2, b : b + width + 2]
    before_grad = (hidden_grad * silu_slope(before)).astype(BF16).astype(F32)
    act_grad = 0.0
    for a in range(3):
        for b in range(3):
            act_grad = act_grad + depth_weight[a * 3 + b] * before_grad[
                2 - a : 2 - a + band, 2 - b : 2 - b + width
            ]
    act_grad = act_grad.astype(BF16).reshape(-1, hidden)
    grads = [act_grad] + [swap(act_grad, "tile", step) for step in range(1, tiles)]

    hidden_act = jax.nn.silu(before[1:-1, 1:-1]).astype(BF16).reshape(-1, hidden)
    adjusted = lax.dot_general(hidden_act, mix_weight, (((1,), (1,)), ((), ())), preferred_element_type=F32)
    adjusted = adjusted.astype(BF16).reshape(1, band, width, hidden)
    mix_term = lax.dot_general(
        upstream.reshape(-1, hidden), hidden_act, (((0,), (0,)), ((), ())), preferred_element_type=F32
    )
    inner_grad = before_grad[1:-1, 1:-1]
    depth_term = jnp.stack(
        [
            jnp.sum(mixed[1 + a : 1 + a + band, 1 + b : 1 + b + width] * inner_grad, axis=(0, 1))
            for a in range(3)
            for b in range(3)
        ]
    )
    rows = hidden // (tiles * cols * reps)
    parts = mix_term.reshape(tiles, cols, reps, rows, hidden)
    depth_grad = jnp.pad(depth_term, ((0, 7), (0, 0)))
    for dim, axis in ((2, "rep"), (1, "col"), (0, "tile")):
        parts, depth_grad = scatter_sum(jnp.moveaxis(parts, dim, 0), depth_grad, axis)
    mix_grad, depth_grad = parts, depth_grad[:9]

    whole = jnp.zeros((tiles,) + act_grad.shape, BF16)
    for step, grad in enumerate(grads):
        whole = lax.dynamic_update_index_in_dim(whole, grad, tile ^ step, 0)
    whole = whole.reshape(-1, hidden)
    in_term = lax.dot_general(own_features, whole, (((0,), (0,)), ((), ())), preferred_element_type=F32)
    in_grad = full_sum(in_term).astype(F32)
    feature_grad = lax.dot_general(
        whole, mixing_input_weight, (((1,), (1,)), ((), ())), preferred_element_type=F32
    ).astype(BF16)
    feature_grad = feature_grad.reshape(height, width, slots, channels).transpose(2, 0, 1, 3)
    slope = jnp.where(live, silu_slope(gate[:, :, 2:-2]), 0.0)
    inner = (feature_grad.astype(F32) * slope).astype(BF16).reshape(slots, -1, channels)
    patches = columns[:, :, 2:-2].reshape(slots, height * width, -1)
    group_term = jnp.einsum("knd,knp->kdp", inner, patches, preferred_element_type=F32)
    group_grad = full_sum(group_term.reshape(slots * channels, -1)).reshape(slots, channels, -1)
    group_grad = jnp.swapaxes(group_grad, 1, 2).astype(F32)
    return (adjusted, mix_grad, depth_grad, in_grad, group_grad)


def solution(mesh):
    in_specs = (
        P(("groups", "rep"), "tile", None, "col"),
        P("tile", None, None),
        P("tile"),
        P("tile", None),
        P(),
        P(),
        P(("groups", "rep"), "tile", "col", None),
    )
    out_specs = (
        P(("groups", "rep"), "tile", "col", None),
        P(("groups", "tile", "col", "rep"), None),
        P("groups", None),
        P(("groups", "tile"), None),
        P(("groups", "tile"), None, None),
    )
    return jax.shard_map(local, mesh=mesh, in_specs=in_specs, out_specs=out_specs, check_vma=False)
```

```python
import functools

import jax
import jax.numpy as jnp
from jax import lax
from jax.experimental import pallas as pl
from jax.experimental.pallas import tpu as pltpu
from jax.sharding import PartitionSpec as P

F32 = jnp.float32
BF16 = jnp.bfloat16
LANES = 128
ROWS = 8
VMEM = pl.BlockSpec(memory_space=pltpu.VMEM)
SMEM = pl.BlockSpec(memory_space=pltpu.SMEM)


def swap(value, axis, step):
    return lax.ppermute(value, axis, [(i, i ^ step) for i in range(lax.axis_size(axis))])


def exchange(low, high, axis):
    count = lax.axis_size(axis)
    even = lax.axis_index(axis) % 2 == 0

    def send(value, first):
        pairs = [(i, i + 1) for i in range(first, count - 1, 2)]
        return lax.ppermute(value, axis, pairs + [(b, a) for a, b in pairs])

    near = send(jnp.where(even, high, low), 0)
    far = send(jnp.where(even, low, high), 1) if count > 2 else None
    return even, near, far


def edges(low, high, axis):
    even, near, far = exchange(low, high, axis)
    if far is None:
        far = jnp.zeros_like(near)
    return jnp.where(even, far, near), jnp.where(even, near, far)


def tree_sum(terms):
    while len(terms) > 1:
        terms = [a + b for a, b in zip(terms[::2], terms[1::2])] + terms[len(terms) & ~1 :]
    return terms[0]


def scatter_sum(parts, extra, axis):
    mine = lax.axis_index(axis)
    size = parts.shape[1:]
    totals, extras = [lax.dynamic_index_in_dim(parts, mine, 0, False)], [extra.astype(BF16).astype(F32)]
    for step in range(1, lax.axis_size(axis)):
        part = lax.dynamic_index_in_dim(parts, mine ^ step, 0, False)
        flat = jnp.concatenate([part.reshape(-1, size[-1]), extra], axis=0).astype(BF16)
        flat = swap(flat, axis, step).astype(F32)
        rows = flat.shape[0] - extra.shape[0]
        totals.append(flat[:rows].reshape(size))
        extras.append(flat[rows:])
    return tree_sum(totals), tree_sum(extras)


def full_sum(keep, send):
    total = (keep.astype(F32) + swap(send, "rep", 1).astype(F32)).astype(BF16)
    step = 1
    while step < lax.axis_size("col"):
        total = (total.astype(F32) + swap(total, "col", step).astype(F32)).astype(BF16)
        step *= 2
    remote = swap(total, "rep", 1)
    first = lax.axis_index("rep") == 0
    return jnp.concatenate([jnp.where(first, total, remote), jnp.where(first, remote, total)], axis=0)


def weight_pieces(weight):
    rows = weight.shape[0]
    piece = (lax.axis_index("col") % 2) * 2 + lax.axis_index("rep")
    blocks = lax.dynamic_slice_in_dim(weight, piece * (rows // 4), rows // 4, axis=0)[None]
    step = 1
    while step < lax.axis_size("tile"):
        blocks = jnp.concatenate([blocks, swap(blocks, "tile", step)], axis=0)
        step *= 2
    across = swap(blocks, "col", 1)
    return piece, [blocks, swap(blocks, "rep", 1), across, swap(across, "rep", 1)]


def silu_slope(value):
    sig = 1.0 / (1.0 + jnp.exp(-value))
    return sig * (1.0 + value * (1.0 - sig))


def lane_below(shape, bound):
    return lax.broadcasted_iota(jnp.int32, shape, len(shape) - 1) < bound


def interleave(first, second):
    half = LANES // 2
    low = lane_below(first.shape, half)
    axis = first.ndim - 1
    return (
        jnp.where(low, first, pltpu.roll(second, half, axis)),
        jnp.where(low, pltpu.roll(first, half, axis), second),
    )


def window_rows(field_ref, near, far, even, slot):
    left, right = jnp.where(even, far, near), jnp.where(even, near, far)
    whole = jnp.concatenate([left, field_ref[slot].astype(F32), right], axis=1)
    half = LANES // 2
    tiles = [whole[:, i : i + LANES] for i in range(0, whole.shape[1], LANES)]
    low = lane_below(tiles[0].shape, half)
    tiles = [pltpu.roll(t, half, 1) for t in tiles]
    middle = jnp.concatenate([jnp.where(low, a, b) for a, b in zip(tiles, tiles[1:])], axis=1)
    height = middle.shape[0]
    row = lax.broadcasted_iota(jnp.int32, middle.shape, 0)
    above = jnp.where(row == 0, 0.0, pltpu.roll(middle, 1, 0))
    below = jnp.where(row == height - 1, 0.0, pltpu.roll(middle, height - 1, 0))
    return above, middle, below


def pair_weight(kernel_ref, slot):
    weight = kernel_ref[slot]
    twice = jnp.concatenate([weight, weight], axis=1)
    span = weight.shape[0] // 3
    blank = jnp.zeros((LANES // 2, LANES), twice.dtype)
    low = lane_below((span + LANES // 2, LANES), LANES // 2)
    parts = []
    for a in range(3):
        part = twice[a * span : (a + 1) * span]
        parts.append(
            jnp.where(low, jnp.concatenate([part, blank], axis=0), jnp.concatenate([blank, part], axis=0))
        )
    return jnp.concatenate(parts, axis=0)


def slot_inputs(scalars, field_ref, kernel_ref, halo_refs, slot):
    even = scalars[2] != 0
    near = halo_refs[0][slot].astype(F32)
    far = halo_refs[1][slot].astype(F32) if len(halo_refs) > 1 else jnp.zeros_like(near)
    return window_rows(field_ref, near, far, even, slot), pair_weight(kernel_ref, slot)


def gate_of(shifted, weight):
    shifted = [s.astype(BF16) for s in shifted]
    pairs = shifted[0].shape[1] // LANES - 1
    lhs = jnp.concatenate(
        [
            jnp.concatenate([s[:, p * LANES : (p + 2) * LANES] for s in shifted], axis=1)
            for p in range(pairs)
        ],
        axis=0,
    )
    gate = jnp.dot(lhs, weight, preferred_element_type=F32)
    return gate.reshape(pairs, -1, LANES)


def halo_rows(pairs):
    return -(-ROWS * (-(-pairs // 2)) // 16) * 16


def send_rows(slots, pairs):
    unit = ROWS * pairs + halo_rows(pairs)
    return unit * slots


def features_kernel(tiles, scalars, field_ref, kernel_ref, *refs):
    halo_refs, out_refs, store = refs[: -tiles - 1], refs[-tiles - 1 : -1], refs[-1]
    slots, height, lanes = field_ref.shape
    pairs = lanes // LANES + 2
    main, halo = ROWS * pairs, halo_rows(pairs)
    tile = scalars[0]

    def values(slot):
        shifted, weight = slot_inputs(scalars, field_ref, kernel_ref, halo_refs, slot)
        gate = gate_of(shifted, weight)
        value = gate / (1.0 + jnp.exp(-gate))
        live = slot < scalars[1]
        first = jnp.where(live & (scalars[3] != 0), value[:1], 0.0)
        last = jnp.where(live & (scalars[4] != 0), value[-1:], 0.0)
        return jnp.concatenate([first, jnp.where(live, value[1:-1], 0.0), last], axis=0)

    def put(value, main_at, halo_at):
        bands = [value[:, ROWS * j : ROWS * (j + 1)] for j in range(height // ROWS)]
        none = jnp.zeros_like(bands[0])
        sub = lax.broadcasted_iota(jnp.int32, none.shape, 1)
        for j, band in enumerate(bands):
            store[j, main_at : main_at + main, :] = band.reshape(main, LANES).astype(BF16)
            above = bands[j - 1] if j else none
            below = bands[j + 1] if j + 1 < len(bands) else none
            both = jnp.where(sub >= 4, above, below)
            tiles_out = []
            for q in range(0, pairs, 2):
                tile_even = pltpu.roll(both[q], 2, 0)
                tile_odd = pltpu.roll(both[q + 1], 6, 0) if q + 1 < pairs else none[0]
                tiles_out.append(jnp.where(sub[0] < 4, tile_even, tile_odd))
            packed = jnp.concatenate(tiles_out, axis=0)
            if packed.shape[0] < halo:
                packed = jnp.concatenate(
                    [packed, jnp.zeros((halo - packed.shape[0], LANES), F32)], axis=0
                )
            store[j, halo_at : halo_at + halo, :] = packed.astype(BF16)

    at = 0
    for slot in range(0, slots - 1, 2):
        even, odd = interleave(values(slot), values(slot + 1))
        put(even, at, at + 2 * main)
        put(odd, at + main, at + 2 * main + halo)
        at += 2 * (main + halo)
    if slots % 2:
        put(values(slots - 1), at, at + main)
    for step, out in enumerate(out_refs):
        out[...] = store[lax.bitwise_xor(tile, step)]


def backward_inputs_kernel(scalars, field_ref, kernel_ref, *refs):
    halo_refs, (patch_ref, slope_ref, own_ref) = refs[:-3], refs[-3:]
    slots, height, lanes = field_ref.shape
    pairs = lanes // LANES
    bands = height // ROWS

    def by_band(value):
        return jnp.concatenate([value[:, ROWS * j : ROWS * (j + 1)] for j in range(bands)], axis=0)

    def values(slot):
        shifted, weight = slot_inputs(scalars, field_ref, kernel_ref, halo_refs, slot)
        gate = gate_of(shifted, weight)[1:-1]
        live = slot < scalars[1]
        slope = by_band(jnp.where(live, silu_slope(gate), 0.0))
        slope_ref[slot] = slope.reshape(-1, LANES).astype(BF16)
        for a, s in enumerate(shifted):
            patch = jnp.concatenate(
                [
                    s[ROWS * j : ROWS * (j + 1), p * LANES : (p + 2) * LANES]
                    for j in range(bands)
                    for p in range(1, pairs + 1)
                ],
                axis=0,
            )
            patch_ref[slot, :, 2 * a * LANES : 2 * (a + 1) * LANES] = patch.astype(BF16)
        return jnp.where(live, gate / (1.0 + jnp.exp(-gate)), 0.0)

    def put(even, odd, lane_tile):
        span = ROWS * pairs
        for j in range(bands):
            for half, value in enumerate((even, odd)):
                rows = value[:, ROWS * j : ROWS * (j + 1)].reshape(span, LANES)
                own_ref[
                    (2 * j + half) * span : (2 * j + half + 1) * span,
                    lane_tile * LANES : (lane_tile + 1) * LANES,
                ] = rows.astype(BF16)

    for slot in range(0, slots - 1, 2):
        put(*interleave(values(slot), values(slot + 1)), slot // 2)
    if slots % 2:
        last = values(slots - 1)
        put(*interleave(last, jnp.zeros_like(last)), slots // 2)


def upstream_kernel(scalars, main_ref, left_ref, right_ref, top_ref, bottom_ref, mix_ref, *refs):
    piece_refs, (grad_ref, weight_ref, rows_ref) = refs[:4], refs[4:]
    width = grad_ref.shape[0] - 2
    cells, hidden = main_ref.shape
    rows_ref[...] = jnp.zeros_like(rows_ref)
    places = (0, cells, cells + 16, cells + 32, cells + 64)
    for place, ref in zip(places, (main_ref, left_ref, right_ref, top_ref, bottom_ref)):
        rows_ref[place : place + ref.shape[0], :] = ref[...]
    shape = ((width + 2) * 16, rows_ref.shape[0])
    target = lax.broadcasted_iota(jnp.int32, shape, 0)
    source = lax.broadcasted_iota(jnp.int32, shape, 1)
    column, row = lax.shift_right_logical(target, 4), target & 15
    want = (row - 1) * width + (column - 1)
    want = jnp.where(column == 0, places[1] + row - 1, want)
    want = jnp.where(column == width + 1, places[2] + row - 1, want)
    want = jnp.where(row == 0, places[3] + column, want)
    want = jnp.where(row == ROWS + 1, places[4] + column, want)
    want = jnp.where(row > ROWS + 1, -1, want)
    pick = jnp.where(source == want, 1.0, 0.0).astype(BF16)
    picked = jnp.dot(pick, rows_ref[...], preferred_element_type=F32).astype(BF16)
    grad = jnp.dot(picked, mix_ref[...], preferred_element_type=F32)
    grad_ref[...] = grad.reshape(width + 2, 16, hidden)
    rows = piece_refs[0].shape[1]
    for number, ref in enumerate(piece_refs):
        start = pl.multiple_of(lax.bitwise_xor(scalars[0], number) * rows, 16)
        weight_ref[:, pl.ds(start, rows), :] = ref[...]


def middle_kernel(tiles, slots, weight_ref, grad_ref, depth_ref, *refs):
    feature_refs = refs[:tiles]
    act_grad_ref, hidden_ref, depth_grad_ref, act, inner = refs[tiles:]
    width = grad_ref.shape[0] - 2
    hidden = weight_ref.shape[2]
    pairs = width // 2 + 2
    main, halo = ROWS * pairs, halo_rows(pairs)
    unit = main + halo
    channels = LANES // 2
    total = None
    for k in range(tiles):
        for s in range(slots // 2):
            term = jnp.dot(
                feature_refs[k][2 * unit * s : 2 * unit * (s + 1), :],
                weight_ref[k, LANES * s : LANES * (s + 1), :],
                preferred_element_type=F32,
            )
            total = term if total is None else total + term
    if slots % 2:
        at = unit * (slots - 1)
        from_slot = channels * (slots - 1)
        for k in range(0, tiles, 2):
            even, odd = interleave(
                feature_refs[k][at : at + unit, :].astype(F32), feature_refs[k + 1][at : at + unit, :].astype(F32)
            )
            lhs = jnp.concatenate([even[:main], odd[:main], even[main:], odd[main:]], axis=0).astype(BF16)
            rhs = jnp.concatenate(
                [weight_ref[k, from_slot:, :], weight_ref[k + 1, from_slot:, :]], axis=0
            )
            total = total + jnp.dot(lhs, rhs, preferred_element_type=F32)
    total = total.astype(BF16).astype(F32)
    for p in range(pairs):
        for half in range(2):
            column = 2 * p + half
            start = half * main + ROWS * p
            act[column, 2 : 2 + ROWS, :] = total[start : start + ROWS]
            start = 2 * main + half * halo + 4 * p
            act[column, 0:2, :] = total[start : start + 2]
            act[column, 2 + ROWS : 4 + ROWS, :] = total[start + 2 : start + 4]

    taps = [(a, b) for a in range(3) for b in range(3)]
    for lane in range(0, hidden, LANES):
        here = slice(lane, lane + LANES)

        def forward(column, carry):
            before = None
            for a, b in taps:
                term = depth_ref[3 * a + b : 3 * a + b + 1, here] * act[column + b, a : a + ROWS + 2, here]
                before = term if before is None else before + term
            sig = 1.0 / (1.0 + jnp.exp(-before))
            slope = sig * (1.0 + before * (1.0 - sig))
            grad = grad_ref[column, 0 : ROWS + 2, here] * slope
            inner[column, 0 : ROWS + 2, here] = grad.astype(BF16).astype(F32)
            hidden_ref[column, :, here] = (before * sig)[1 : ROWS + 1].astype(BF16)
            return carry

        lax.fori_loop(0, width + 2, forward, 0)

        def backward(column, sums):
            grad = None
            for a, b in taps:
                term = depth_ref[3 * a + b : 3 * a + b + 1, here] * inner[column + 2 - b, 2 - a : 2 - a + ROWS, here]
                grad = term if grad is None else grad + term
            place = lax.shift_right_logical(column, 1) + (column & 1) * (width // 2)
            act_grad_ref[place, :, here] = grad.astype(BF16)
            own = inner[column + 1, 1 : 1 + ROWS, here]
            return tuple(
                total + act[column + 1 + b, 1 + a : 1 + a + ROWS, here] * own
                for (a, b), total in zip(taps, sums)
            )

        zero = jnp.zeros((ROWS, LANES), F32)
        sums = lax.fori_loop(0, width, backward, (zero,) * 9)
        for tap, value in enumerate(sums):
            depth_grad_ref[tap : tap + 1, here] = jnp.sum(value, axis=0, keepdims=True)


def gradients_kernel(tiles, scalars, weight_ref, own_ref, slope_ref, patch_ref, *refs):
    grad_refs = refs[:tiles]
    in_keep, in_send, group_keep, group_send, whole, in_term, group_term = refs[tiles:]
    slots, span, lanes = patch_ref.shape
    channels = LANES // 2
    cells = grad_refs[0].shape[0]
    for step, ref in enumerate(grad_refs):
        start = pl.multiple_of(lax.bitwise_xor(scalars[0], step) * cells, 16)
        whole[pl.ds(start, cells), :] = ref[...]
    rows = whole[...]
    rep = scalars[1]
    term = lax.dot_general(own_ref[...], rows, (((0,), (0,)), ((), ())), preferred_element_type=F32)
    half = in_keep.shape[0]
    in_term[...] = term[: 2 * half].astype(BF16)
    in_keep[...] = in_term[pl.ds(pl.multiple_of(rep * half, 16), half), :]
    in_send[...] = in_term[pl.ds(pl.multiple_of((1 - rep) * half, 16), half), :]

    feature_grad = lax.dot_general(rows, weight_ref[...], (((1,), (1,)), ((), ())), preferred_element_type=F32)
    feature_grad = feature_grad.astype(BF16).astype(F32)
    blank = slots * channels % LANES
    if blank:
        feature_grad = jnp.concatenate(
            [feature_grad, jnp.zeros((feature_grad.shape[0], LANES - blank), F32)], axis=1
        )
    part = cells // 2

    def halves(value):
        return [
            jnp.concatenate(
                [value[cells * j + part * h : cells * j + part * (h + 1)] for j in range(tiles)], axis=0
            )
            for h in range(2)
        ]

    for slot in range(0, slots, 2):
        tile = feature_grad[:, slot * channels : slot * channels + LANES]
        both = interleave(*halves(tile))
        for k in range(slot, min(slot + 2, slots)):
            inner = (both[k - slot] * slope_ref[k].astype(F32)).astype(BF16)
            term = lax.dot_general(inner, patch_ref[k], (((0,), (0,)), ((), ())), preferred_element_type=F32)
            quarter = lanes // 3
            use = 3 * channels
            low = jnp.concatenate([term[:channels, quarter * a : quarter * a + use] for a in range(3)], axis=1)
            high = jnp.concatenate(
                [term[channels:, quarter * a + channels : quarter * (a + 1)] for a in range(3)], axis=1
            )
            group_term[channels * k : channels * (k + 1), :] = (low + high).astype(BF16)
    half = group_keep.shape[0]
    group_keep[...] = group_term[pl.ds(pl.multiple_of(rep * half, 16), half), :]
    group_send[...] = group_term[pl.ds(pl.multiple_of((1 - rep) * half, 16), half), :]


def call(kernel, outs, operands, scratch=(), flops=1 << 24):
    shapes = [jax.ShapeDtypeStruct(s, d) for s, d in outs]
    scalars = jnp.issubdtype(operands[0].dtype, jnp.integer)
    moved = sum(o.size * o.dtype.itemsize for o in list(operands) + shapes)
    return pl.pallas_call(
        kernel,
        out_shape=shapes,
        in_specs=[SMEM if scalars and i == 0 else VMEM for i in range(len(operands))],
        out_specs=[VMEM] * len(shapes),
        scratch_shapes=list(scratch),
        cost_estimate=pl.CostEstimate(flops=flops, bytes_accessed=moved, transcendentals=0),
    )(*operands)


def local(
    forcing,
    member_kernel_weight,
    member_counts,
    mixing_input_weight,
    depth_weight,
    mix_weight,
    cotangent,
):
    channels = member_kernel_weight.shape[2]
    slots = forcing.shape[1]
    height = forcing.shape[2]
    width = forcing.shape[3] // channels
    hidden = mixing_input_weight.shape[1]
    tiles, cols, reps = (lax.axis_size(a) for a in ("tile", "col", "rep"))
    tile, col, rep = (lax.axis_index(a) for a in ("tile", "col", "rep"))
    pairs = width // 2 + 2
    cells = ROWS * width
    assert height == ROWS * tiles and 2 * channels == LANES

    field = forcing[0]
    reach = 4 * channels
    even, near, far = exchange(field[..., :reach], field[..., -reach:], "col")
    halos = [near] if far is None else [near, far]
    scalars = jnp.stack(
        [tile, member_counts[0], even.astype(jnp.int32), (col > 0).astype(jnp.int32), (col < cols - 1).astype(jnp.int32)]
    )
    rows = send_rows(slots, pairs)
    sent = call(
        functools.partial(features_kernel, tiles),
        [((rows, LANES), BF16)] * tiles,
        [scalars, field, member_kernel_weight, *halos],
        [pltpu.VMEM((tiles, rows, LANES), BF16)],
    )
    pieces = [swap(piece, "tile", step) if step else piece for step, piece in enumerate(sent)]

    patch, slope, own_features = call(
        backward_inputs_kernel,
        [
            ((slots, cells // 2 * tiles, 6 * LANES), BF16),
            ((slots, cells // 2 * tiles, LANES), BF16),
            ((cells * tiles, -(-slots // 2) * LANES), BF16),
        ],
        [scalars, field, member_kernel_weight, *halos],
    )

    number, blocks = weight_pieces(mixing_input_weight)
    upstream = cotangent[0]
    left, right = edges(upstream[:, :1], upstream[:, -1:], "col")
    wide = jnp.concatenate([left, upstream, right], axis=1)
    top, bottom = edges(wide[:1], wide[-1:], "tile")
    flat_upstream = upstream.reshape(cells, hidden)
    hidden_grad, weight = call(
        upstream_kernel,
        [((width + 2, 16, hidden), F32), ((tiles,) + mixing_input_weight.shape, BF16)],
        [number[None], flat_upstream, left[:, 0], right[:, 0], top[0], bottom[0], mix_weight, *blocks],
        [pltpu.VMEM((2 * LANES, hidden), BF16)],
    )

    act_grad, hidden_act, depth_term = call(
        functools.partial(middle_kernel, tiles, slots),
        [((width, ROWS, hidden), BF16), ((width + 2, ROWS, hidden), BF16), ((16, hidden), F32)],
        [weight, hidden_grad, depth_weight, *pieces],
        [pltpu.VMEM((width + 4, 16, hidden), F32), pltpu.VMEM((width + 2, 16, hidden), F32)],
    )
    act_grad = act_grad.reshape(cells, hidden)
    grads = [act_grad] + [swap(act_grad, "tile", step) for step in range(1, tiles)]

    hidden_act = hidden_act[1:-1].transpose(1, 0, 2).reshape(cells, hidden)
    adjusted = lax.dot_general(hidden_act, mix_weight, (((1,), (1,)), ((), ())), preferred_element_type=F32)
    adjusted = adjusted.astype(BF16).reshape(1, ROWS, width, hidden)
    mix_term = lax.dot_general(
        flat_upstream, hidden_act, (((0,), (0,)), ((), ())), preferred_element_type=F32
    )
    parts = mix_term.reshape(tiles, cols, reps, -1, hidden)
    depth_grad = jnp.where(jnp.arange(16)[:, None] < 9, depth_term, 0.0)
    for dim, axis in ((2, "rep"), (1, "col"), (0, "tile")):
        parts, depth_grad = scatter_sum(jnp.moveaxis(parts, dim, 0), depth_grad, axis)
    mix_grad, depth_grad = parts, depth_grad[:9]

    half = slots * channels // 2
    in_half, group_half = ((half, hidden), BF16), ((half, 9 * channels), BF16)
    in_keep, in_send, group_keep, group_send = call(
        functools.partial(gradients_kernel, tiles),
        [in_half, in_half, group_half, group_half],
        [jnp.stack([tile, rep]), mixing_input_weight, own_features, slope, patch, *grads],
        [
            pltpu.VMEM((cells * tiles, hidden), BF16),
            pltpu.VMEM((2 * half, hidden), BF16),
            pltpu.VMEM((2 * half, 9 * channels), BF16),
        ],
    )
    in_grad = full_sum(in_keep, in_send).astype(F32)
    group_grad = full_sum(group_keep, group_send).reshape(slots, channels, -1)
    group_grad = jnp.swapaxes(group_grad, 1, 2).astype(F32)
    return (adjusted, mix_grad, depth_grad, in_grad, group_grad)


def solution(mesh):
    in_specs = (
        P(("groups", "rep"), "tile", None, "col"),
        P("tile", None, None),
        P("tile"),
        P("tile", None),
        P(),
        P(),
        P(("groups", "rep"), "tile", "col", None),
    )
    out_specs = (
        P(("groups", "rep"), "tile", "col", None),
        P(("groups", "tile", "col", "rep"), None),
        P("groups", None),
        P(("groups", "tile"), None),
        P(("groups", "tile"), None, None),
    )
    return jax.shard_map(local, mesh=mesh, in_specs=in_specs, out_specs=out_specs, check_vma=False)
```

```python
import functools

import jax
import jax.numpy as jnp
from jax import lax
from jax.experimental import pallas as pl
from jax.experimental.pallas import tpu as pltpu
from jax.sharding import PartitionSpec as P

F32 = jnp.float32
BF16 = jnp.bfloat16
LANES = 128
ROWS = 8
VMEM = pl.BlockSpec(memory_space=pltpu.VMEM)
SMEM = pl.BlockSpec(memory_space=pltpu.SMEM)


def swap(value, axis, step):
    return lax.ppermute(value, axis, [(i, i ^ step) for i in range(lax.axis_size(axis))])


def neighbours(value_at, axis):
    count = lax.axis_size(axis)
    even = lax.axis_index(axis) % 2 == 0

    def send(value, first):
        pairs = [(i, i + 1) for i in range(first, count - 1, 2)]
        return lax.ppermute(value, axis, pairs + [(b, a) for a, b in pairs])

    near = send(value_at(even), 0)
    far = send(value_at(~even), 1) if count > 2 else None
    return even, near, far


def edges(value, axis, dim):
    def value_at(last):
        start = jnp.where(last, value.shape[dim] - 1, 0)
        return lax.dynamic_slice_in_dim(value, start, 1, dim)

    even, near, far = neighbours(value_at, axis)
    if far is None:
        far = jnp.zeros_like(near)
    return jnp.where(even, far, near), jnp.where(even, near, far)


def tree_sum(terms):
    while len(terms) > 1:
        terms = [a + b for a, b in zip(terms[::2], terms[1::2])] + terms[len(terms) & ~1 :]
    return terms[0]


def scatter_sum(parts, extra, axis):
    mine = lax.axis_index(axis)
    size = parts.shape[1:]
    totals, extras = [lax.dynamic_index_in_dim(parts, mine, 0, False)], [extra.astype(BF16).astype(F32)]
    for step in range(1, lax.axis_size(axis)):
        part = lax.dynamic_index_in_dim(parts, mine ^ step, 0, False)
        flat = jnp.concatenate([part.reshape(-1, size[-1]), extra], axis=0).astype(BF16)
        flat = swap(flat, axis, step).astype(F32)
        rows = flat.shape[0] - extra.shape[0]
        totals.append(flat[:rows].reshape(size))
        extras.append(flat[rows:])
    return tree_sum(totals), tree_sum(extras)


def full_sum(keep, send):
    total = (keep.astype(F32) + swap(send, "rep", 1).astype(F32)).astype(BF16)
    step = 1
    while step < lax.axis_size("col"):
        total = (total.astype(F32) + swap(total, "col", step).astype(F32)).astype(BF16)
        step *= 2
    remote = swap(total, "rep", 1)
    first = lax.axis_index("rep") == 0
    return jnp.concatenate([jnp.where(first, total, remote), jnp.where(first, remote, total)], axis=0)


def silu_slope(value):
    sig = 1.0 / (1.0 + jnp.exp(-value))
    return sig * (1.0 + value * (1.0 - sig))


def lane_below(shape, bound):
    return lax.broadcasted_iota(jnp.int32, shape, len(shape) - 1) < bound


def interleave(first, second):
    half = LANES // 2
    low = lane_below(first.shape, half)
    axis = first.ndim - 1
    return (
        jnp.where(low, first, pltpu.roll(second, half, axis)),
        jnp.where(low, pltpu.roll(first, half, axis), second),
    )


def window_rows(field_ref, near, far, even, slot):
    left, right = jnp.where(even, far, near), jnp.where(even, near, far)
    whole = jnp.concatenate([left, field_ref[slot].astype(F32), right], axis=1)
    half = LANES // 2
    tiles = [whole[:, i : i + LANES] for i in range(0, whole.shape[1], LANES)]
    low = lane_below(tiles[0].shape, half)
    tiles = [pltpu.roll(t, half, 1) for t in tiles]
    middle = jnp.concatenate([jnp.where(low, a, b) for a, b in zip(tiles, tiles[1:])], axis=1)
    height = middle.shape[0]
    row = lax.broadcasted_iota(jnp.int32, middle.shape, 0)
    above = jnp.where(row == 0, 0.0, pltpu.roll(middle, 1, 0))
    below = jnp.where(row == height - 1, 0.0, pltpu.roll(middle, height - 1, 0))
    return above, middle, below


def pair_weight(kernel_ref, slot):
    weight = kernel_ref[slot].astype(F32)
    span = weight.shape[1] // 3
    parts = [weight[:, a * span : (a + 1) * span] for a in range(3)]
    blank = jnp.zeros((weight.shape[0], LANES // 2), F32)
    first = jnp.concatenate([x for part in parts for x in (part, blank)], axis=1)
    second = jnp.concatenate([x for part in parts for x in (blank, part)], axis=1)
    return jnp.concatenate([first, second], axis=0).astype(BF16)


def slot_inputs(field_ref, kernel_ref, halo_refs, slot):
    even = lax.rem(lax.axis_index("col"), 2) == 0
    near = halo_refs[0][slot].astype(F32)
    far = halo_refs[1][slot].astype(F32) if len(halo_refs) > 1 else jnp.zeros_like(near)
    return window_rows(field_ref, near, far, even, slot), pair_weight(kernel_ref, slot)


def gate_of(shifted, weight):
    shifted = [s.astype(BF16) for s in shifted]
    pairs = shifted[0].shape[1] // LANES - 1
    lhs = jnp.concatenate(
        [
            jnp.concatenate([s[:, p * LANES : (p + 2) * LANES] for s in shifted], axis=1)
            for p in range(pairs)
        ],
        axis=0,
    )
    gate = lax.dot_general(lhs, weight, (((1,), (1,)), ((), ())), preferred_element_type=F32)
    return gate.reshape(pairs, -1, LANES)


def features_kernel(tiles, count_ref, field_ref, kernel_ref, weight_ref, *refs):
    halo_refs, out_refs, store = refs[: -tiles - 1], refs[-tiles - 1 : -1], refs[-1]
    slots, height, lanes = field_ref.shape
    pairs = lanes // LANES + 2
    main = ROWS * pairs
    col = lax.axis_index("col")

    def values(slot):
        shifted, weight = slot_inputs(field_ref, kernel_ref, halo_refs, slot)
        gate = gate_of(shifted, weight)
        value = gate / (1.0 + jnp.exp(-gate))
        live = slot < count_ref[0]
        first = jnp.where(live & (col > 0), value[:1], 0.0)
        last = jnp.where(live & (col < lax.axis_size("col") - 1), value[-1:], 0.0)
        return jnp.concatenate([first, jnp.where(live, value[1:-1], 0.0), last], axis=0)

    def around(bands, j):
        none = jnp.zeros_like(bands[0])
        sub = lax.broadcasted_iota(jnp.int32, none.shape, 1)
        both = jnp.where(sub >= 4, bands[j - 1] if j else none, bands[j + 1] if j + 1 < len(bands) else none)
        packed = [
            jnp.where(sub[0] < 4, pltpu.roll(both[q], 2, 0), pltpu.roll(both[q + 1], 6, 0))
            for q in range(0, pairs, 2)
        ]
        return jnp.concatenate(packed, axis=0)

    def put(both, lane_tile):
        here = slice(lane_tile * LANES, (lane_tile + 1) * LANES)
        bands = [[v[:, ROWS * j : ROWS * (j + 1)] for j in range(height // ROWS)] for v in both]
        for j in range(height // ROWS):
            for half in range(2):
                rows = bands[half][j].reshape(main, LANES)
                store[j, half * main : (half + 1) * main, here] = rows.astype(BF16)
            halo = jnp.concatenate([around(bands[half], j) for half in range(2)], axis=0)
            store[j, 2 * main :, here] = halo.astype(BF16)

    for slot in range(0, slots - 1, 2):
        put(interleave(values(slot), values(slot + 1)), slot // 2)
    if slots % 2:
        last = values(slots - 1)
        put(interleave(last, jnp.zeros_like(last)), slots // 2)
    depth = weight_ref.shape[0]
    whole = depth // LANES * LANES
    for step, out in enumerate(out_refs):
        band = lax.bitwise_xor(lax.axis_index("tile"), step)
        term = jnp.dot(store[band, :, :whole], weight_ref[:whole, :], preferred_element_type=F32)
        if depth > whole:
            rest = jnp.concatenate(
                [weight_ref[whole:, :], jnp.zeros((LANES - depth + whole, weight_ref.shape[1]), BF16)], axis=0
            )
            term += jnp.dot(store[band, :, whole:], rest, preferred_element_type=F32)
        out[...] = term.astype(BF16)


def backward_inputs_kernel(count_ref, field_ref, kernel_ref, *refs):
    halo_refs, (patch_ref, slope_ref, own_ref) = refs[:-3], refs[-3:]
    slots, height, lanes = field_ref.shape
    pairs = lanes // LANES
    bands = height // ROWS

    def by_band(value):
        return jnp.concatenate([value[:, ROWS * j : ROWS * (j + 1)] for j in range(bands)], axis=0)

    def values(slot):
        shifted, weight = slot_inputs(field_ref, kernel_ref, halo_refs, slot)
        gate = gate_of(shifted, weight)[1:-1]
        live = slot < count_ref[0]
        slope = by_band(jnp.where(live, silu_slope(gate), 0.0))
        slope_ref[slot] = slope.reshape(-1, LANES).astype(BF16)
        for a, s in enumerate(shifted):
            patch = jnp.concatenate(
                [
                    s[ROWS * j : ROWS * (j + 1), p * LANES : (p + 2) * LANES]
                    for j in range(bands)
                    for p in range(1, pairs + 1)
                ],
                axis=0,
            )
            patch_ref[slot, :, 2 * a * LANES : 2 * (a + 1) * LANES] = patch.astype(BF16)
        return jnp.where(live, gate / (1.0 + jnp.exp(-gate)), 0.0)

    def put(even, odd, lane_tile):
        span = ROWS * pairs
        for j in range(bands):
            for half, value in enumerate((even, odd)):
                rows = value[:, ROWS * j : ROWS * (j + 1)].reshape(span, LANES)
                own_ref[
                    (2 * j + half) * span : (2 * j + half + 1) * span,
                    lane_tile * LANES : (lane_tile + 1) * LANES,
                ] = rows.astype(BF16)

    for slot in range(0, slots - 1, 2):
        put(*interleave(values(slot), values(slot + 1)), slot // 2)
    if slots % 2:
        last = values(slots - 1)
        put(*interleave(last, jnp.zeros_like(last)), slots // 2)


def upstream_kernel(main_ref, left_ref, right_ref, top_ref, bottom_ref, mix_ref, grad_ref, rows_ref):
    width = grad_ref.shape[0] - 2
    cells, hidden = main_ref.shape
    rows_ref[...] = jnp.zeros_like(rows_ref)
    places = (0, cells, cells + 16, cells + 32, cells + 64)
    for place, ref in zip(places, (main_ref, left_ref, right_ref, top_ref, bottom_ref)):
        rows_ref[place : place + ref.shape[0], :] = ref[...]
    shape = ((width + 2) * 16, rows_ref.shape[0])
    target = lax.broadcasted_iota(jnp.int32, shape, 0)
    source = lax.broadcasted_iota(jnp.int32, shape, 1)
    column, row = lax.shift_right_logical(target, 4), target & 15
    want = (row - 1) * width + (column - 1)
    want = jnp.where(column == 0, places[1] + row - 1, want)
    want = jnp.where(column == width + 1, places[2] + row - 1, want)
    want = jnp.where(row == 0, places[3] + column, want)
    want = jnp.where(row == ROWS + 1, places[4] + column, want)
    want = jnp.where(row > ROWS + 1, -1, want)
    pick = jnp.where(source == want, 1.0, 0.0).astype(BF16)
    picked = jnp.dot(pick, rows_ref[...], preferred_element_type=F32).astype(BF16)
    grad = jnp.dot(picked, mix_ref[...], preferred_element_type=F32)
    grad_ref[...] = grad.reshape(width + 2, 16, hidden)


TAPS = [(a, b) for a in range(3) for b in range(3)]


def middle_kernel(tiles, grad_ref, depth_ref, *refs):
    term_refs, (act_grad_ref, hidden_ref, act, inner) = refs[:tiles], refs[tiles:]
    width, hidden = grad_ref.shape[0] - 2, grad_ref.shape[2]
    pairs = width // 2 + 2
    main = ROWS * pairs
    chunks = [(n, slice(n * LANES, (n + 1) * LANES)) for n in range(hidden // LANES)]
    for n, here in chunks:
        total = tree_sum([ref[:, here].astype(F32) for ref in term_refs]).astype(BF16).astype(F32)
        for p in range(pairs):
            for half in range(2):
                start = half * main + ROWS * p
                act[n, 2 * p + half, 2 : 2 + ROWS, :] = total[start : start + ROWS]
                start = 2 * main + half * main // 2 + 4 * p
                act[n, 2 * p + half, 0:2, :] = total[start : start + 2]
                act[n, 2 * p + half, 2 + ROWS : 4 + ROWS, :] = total[start + 2 : start + 4]

    def forward(column, carry):
        for n, here in chunks:
            terms = [
                depth_ref[3 * a + b : 3 * a + b + 1, here] * act[n, column + b, a : a + ROWS + 2, :] for a, b in TAPS
            ]
            before = tree_sum(terms)
            sig = 1.0 / (1.0 + jnp.exp(-before))
            slope = sig * (1.0 + before * (1.0 - sig))
            grad = grad_ref[column, 0 : ROWS + 2, here] * slope
            inner[n, column, 0 : ROWS + 2, :] = grad.astype(BF16).astype(F32)
            hidden_ref[column, :, here] = (before * sig)[1 : ROWS + 1].astype(BF16)
        return carry

    lax.fori_loop(0, width + 2, forward, 0)

    def backward(column, carry):
        place = lax.shift_right_logical(column, 1) + (column & 1) * (width // 2)
        for n, here in chunks:
            terms = [
                depth_ref[3 * a + b : 3 * a + b + 1, here] * inner[n, column + 2 - b, 2 - a : 2 - a + ROWS, :]
                for a, b in TAPS
            ]
            act_grad_ref[place, :, here] = tree_sum(terms).astype(BF16)
        return carry

    lax.fori_loop(0, width, backward, 0)


def depth_kernel(act, inner, out_ref):
    chunks, columns = act.shape[:2]

    def add(column, sums):
        new = []
        for n in range(chunks):
            own = inner[n, column + 1, 1 : 1 + ROWS, :]
            for t, (a, b) in enumerate(TAPS):
                new.append(sums[n * 9 + t] + act[n, column + 1 + b, 1 + a : 1 + a + ROWS, :] * own)
        return tuple(new)

    zero = jnp.zeros((ROWS, LANES), F32)
    sums = lax.fori_loop(0, columns - 4, add, (zero,) * (9 * chunks))
    out_ref[...] = jnp.zeros_like(out_ref)
    for n in range(chunks):
        for t in range(9):
            out_ref[t : t + 1, n * LANES : (n + 1) * LANES] = jnp.sum(sums[n * 9 + t], axis=0, keepdims=True)


def in_gradient_kernel(tiles, own_ref, *refs):
    grad_refs, (keep, send, whole, held) = refs[:tiles], refs[tiles:]
    cells = grad_refs[0].shape[0]
    for step, ref in enumerate(grad_refs):
        start = pl.multiple_of(lax.bitwise_xor(lax.axis_index("tile"), step) * cells, 16)
        whole[pl.ds(start, cells), :] = ref[...]
    term = lax.dot_general(own_ref[...], whole[...], (((0,), (0,)), ((), ())), preferred_element_type=F32)
    half = keep.shape[0]
    rep = lax.axis_index("rep")
    held[...] = term[: 2 * half].astype(BF16)
    keep[...] = held[pl.ds(pl.multiple_of(rep * half, 16), half), :]
    send[...] = held[pl.ds(pl.multiple_of((1 - rep) * half, 16), half), :]


def group_gradient_kernel(tiles, rows_ref, weight_ref, slope_ref, patch_ref, group_keep, group_send, group_term):
    slots, span, lanes = patch_ref.shape
    channels = LANES // 2
    rows = rows_ref[...]
    cells = rows.shape[0] // tiles
    rep = lax.axis_index("rep")
    feature_grad = lax.dot_general(rows, weight_ref[...], (((1,), (1,)), ((), ())), preferred_element_type=F32)
    feature_grad = feature_grad.astype(BF16).astype(F32)
    blank = slots * channels % LANES
    if blank:
        feature_grad = jnp.concatenate(
            [feature_grad, jnp.zeros((feature_grad.shape[0], LANES - blank), F32)], axis=1
        )
    part = cells // 2

    def halves(value):
        return [
            jnp.concatenate(
                [value[cells * j + part * h : cells * j + part * (h + 1)] for j in range(tiles)], axis=0
            )
            for h in range(2)
        ]

    for slot in range(0, slots, 2):
        tile = feature_grad[:, slot * channels : slot * channels + LANES]
        both = interleave(*halves(tile))
        for k in range(slot, min(slot + 2, slots)):
            inner = (both[k - slot] * slope_ref[k].astype(F32)).astype(BF16)
            term = lax.dot_general(inner, patch_ref[k], (((0,), (0,)), ((), ())), preferred_element_type=F32)
            quarter = lanes // 3
            use = 3 * channels
            low = jnp.concatenate([term[:channels, quarter * a : quarter * a + use] for a in range(3)], axis=1)
            high = jnp.concatenate(
                [term[channels:, quarter * a + channels : quarter * (a + 1)] for a in range(3)], axis=1
            )
            group_term[channels * k : channels * (k + 1), :] = (low + high).astype(BF16)
    half = group_keep.shape[0]
    group_keep[...] = group_term[pl.ds(pl.multiple_of(rep * half, 16), half), :]
    group_send[...] = group_term[pl.ds(pl.multiple_of((1 - rep) * half, 16), half), :]


def call(kernel, outs, operands, scratch=(), flops=1 << 24):
    shapes = [jax.ShapeDtypeStruct(s, d) for s, d in outs]
    moved = sum(o.size * o.dtype.itemsize for o in list(operands) + shapes)
    return pl.pallas_call(
        kernel,
        out_shape=shapes,
        in_specs=[SMEM if jnp.issubdtype(o.dtype, jnp.integer) else VMEM for o in operands],
        out_specs=[VMEM] * len(shapes),
        scratch_shapes=list(scratch),
        cost_estimate=pl.CostEstimate(flops=flops, bytes_accessed=moved, transcendentals=0),
        compiler_params=pltpu.CompilerParams(vmem_limit_bytes=32 << 20),
    )(*operands)


def local(
    forcing,
    member_kernel_weight,
    member_counts,
    mixing_input_weight,
    depth_weight,
    mix_weight,
    cotangent,
):
    channels = member_kernel_weight.shape[2]
    slots = forcing.shape[1]
    height = forcing.shape[2]
    width = forcing.shape[3] // channels
    hidden = mixing_input_weight.shape[1]
    tiles, cols, reps = (lax.axis_size(a) for a in ("tile", "col", "rep"))
    pairs = width // 2 + 2
    cells = ROWS * width
    assert height == ROWS * tiles and 2 * channels == LANES and pairs % 2 == 0
    kernel_weight = jnp.swapaxes(member_kernel_weight, 1, 2)

    field = forcing[0]
    reach = 4 * channels

    def field_edge(last):
        return lax.dynamic_slice_in_dim(field, jnp.where(last, field.shape[2] - reach, 0), reach, 2)

    _, near, far = neighbours(field_edge, "col")
    halos = [near] if far is None else [near, far]
    sent = call(
        functools.partial(features_kernel, tiles),
        [((3 * ROWS * pairs, hidden), BF16)] * tiles,
        [member_counts, field, kernel_weight, mixing_input_weight, *halos],
        [pltpu.VMEM((tiles, 3 * ROWS * pairs, -(-slots // 2) * LANES), BF16)],
        flops=1 << 28,
    )
    order = sorted(range(1, tiles), key=lambda step: -step)
    received = {step: swap(sent[step], "tile", step) for step in order}
    cotangent, own_term, *halos = lax.optimization_barrier((cotangent, sent[0], *halos))

    upstream = cotangent[0]
    left, right = edges(upstream, "col", 1)
    wide = jnp.concatenate([left, upstream, right], axis=1)
    top, bottom = edges(wide, "tile", 0)
    flat_upstream = upstream.reshape(cells, hidden)
    (hidden_grad,) = call(
        upstream_kernel,
        [((width + 2, 16, hidden), F32)],
        [flat_upstream, left[:, 0], right[:, 0], top[0], bottom[0], mix_weight],
        [pltpu.VMEM((2 * LANES, hidden), BF16)],
        flops=1 << 28,
    )
    patch, slope, own_features = call(
        backward_inputs_kernel,
        [
            ((slots, cells // 2 * tiles, 6 * LANES), BF16),
            ((slots, cells // 2 * tiles, LANES), BF16),
            ((cells * tiles, -(-slots // 2) * LANES), BF16),
        ],
        [member_counts, field, kernel_weight, *halos],
        flops=1 << 28,
    )
    terms = [own_term] + [received[step] for step in range(1, tiles)]
    patch, slope, own_features, hidden_grad, *terms = lax.optimization_barrier(
        (patch, slope, own_features, hidden_grad, *terms)
    )

    act_grad, hidden_act, act, inner = call(
        functools.partial(middle_kernel, tiles),
        [
            ((width, ROWS, hidden), BF16),
            ((width + 2, ROWS, hidden), BF16),
            ((hidden // LANES, width + 4, 16, LANES), F32),
            ((hidden // LANES, width + 2, 16, LANES), F32),
        ],
        [hidden_grad, depth_weight, *terms],
    )
    act_grad = act_grad.reshape(cells, hidden)
    received = {step: swap(act_grad, "tile", step) for step in order}
    grads = [act_grad] + [received[step] for step in range(1, tiles)]

    (depth_term,) = call(depth_kernel, [((16, hidden), F32)], [act, inner])
    hidden_act = hidden_act[1:-1].transpose(1, 0, 2).reshape(cells, hidden)
    adjusted = lax.dot_general(hidden_act, mix_weight, (((1,), (1,)), ((), ())), preferred_element_type=F32)
    adjusted = adjusted.astype(BF16).reshape(1, ROWS, width, hidden)
    mix_term = lax.dot_general(
        flat_upstream, hidden_act, (((0,), (0,)), ((), ())), preferred_element_type=F32
    )
    parts = mix_term.reshape(tiles, cols, reps, -1, hidden)
    depth_grad = depth_term
    for dim, axis in ((2, "rep"), (1, "col")):
        parts, depth_grad = scatter_sum(jnp.moveaxis(parts, dim, 0), depth_grad, axis)
    parts, depth_grad, adjusted, *grads = lax.optimization_barrier((parts, depth_grad, adjusted, *grads))

    half = slots * channels // 2
    in_keep, in_send, rows = call(
        functools.partial(in_gradient_kernel, tiles),
        [((half, hidden), BF16), ((half, hidden), BF16), ((cells * tiles, hidden), BF16)],
        [own_features, *grads],
        [pltpu.VMEM((2 * half, hidden), BF16)],
    )
    group_keep, group_send = call(
        functools.partial(group_gradient_kernel, tiles),
        [((half, 9 * channels), BF16), ((half, 9 * channels), BF16)],
        [rows, mixing_input_weight, slope, patch],
        [pltpu.VMEM((2 * half, 9 * channels), BF16)],
        flops=1 << 28,
    )
    in_grad = full_sum(in_keep, in_send).astype(F32)
    group_grad = full_sum(group_keep, group_send).reshape(slots, channels, -1)
    group_grad = jnp.swapaxes(group_grad, 1, 2).astype(F32)
    mix_grad, depth_grad = scatter_sum(parts, depth_grad, "tile")
    return (adjusted, mix_grad, depth_grad[:9], in_grad, group_grad)


def solution(mesh):
    in_specs = (
        P(("groups", "rep"), "tile", None, "col"),
        P("tile", None, None),
        P("tile"),
        P("tile", None),
        P(),
        P(),
        P(("groups", "rep"), "tile", "col", None),
    )
    out_specs = (
        P(("groups", "rep"), "tile", "col", None),
        P(("groups", "tile", "col", "rep"), None),
        P("groups", None),
        P(("groups", "tile"), None),
        P(("groups", "tile"), None, None),
    )
    return jax.shard_map(local, mesh=mesh, in_specs=in_specs, out_specs=out_specs, check_vma=False)
```

```python
import functools
import math

import jax
import jax.numpy as jnp
from jax import lax
from jax.experimental import pallas as pl
from jax.experimental.pallas import tpu as pltpu
from jax.sharding import PartitionSpec as P


F32 = jnp.float32
BF16 = jnp.bfloat16
LANES = 128
ROWS = 8
VMEM = pl.BlockSpec(memory_space=pltpu.VMEM)
SMEM = pl.BlockSpec(memory_space=pltpu.SMEM)
HBM = pl.BlockSpec(memory_space=pltpu.HBM)


def swap(value, axis, step):
    return lax.ppermute(value, axis, [(i, i ^ step) for i in range(lax.axis_size(axis))])


def with_neighbours(values, axis):
    count = lax.axis_size(axis)
    received = []
    for first, value in enumerate(values):
        pairs = [(i, i + 1) for i in range(first, count - 1, 2)]
        received.append(lax.ppermute(value, axis, pairs + [(b, a) for a, b in pairs]))
    return received


def in_order(received, axis):
    even = lax.axis_index(axis) % 2 == 0
    near = received[0]
    far = received[1] if len(received) > 1 else jnp.zeros_like(near)
    return jnp.where(even, far, near), jnp.where(even, near, far)


def tree_sum(terms):
    while len(terms) > 1:
        terms = [a + b for a, b in zip(terms[::2], terms[1::2])] + terms[len(terms) & ~1 :]
    return terms[0]


def full_sum(keep, send):
    total = (keep.astype(F32) + swap(send, "rep", 1).astype(F32)).astype(BF16)
    step = 1
    while step < lax.axis_size("col"):
        total = (total.astype(F32) + swap(total, "col", step).astype(F32)).astype(BF16)
        step *= 2
    remote = swap(total, "rep", 1)
    first = lax.axis_index("rep") == 0
    return jnp.concatenate([jnp.where(first, total, remote), jnp.where(first, remote, total)], axis=0)


def silu_slope(value):
    sig = 1.0 / (1.0 + jnp.exp(-value))
    return sig * (1.0 + value * (1.0 - sig))


def lane_below(shape, bound):
    return lax.broadcasted_iota(jnp.int32, shape, len(shape) - 1) < bound


def interleave(first, second):
    half = LANES // 2
    low = lane_below(first.shape, half)
    axis = first.ndim - 1
    return (
        jnp.where(low, first, pltpu.roll(second, half, axis)),
        jnp.where(low, pltpu.roll(first, half, axis), second),
    )


def window_rows(field_ref, near, far, even, slot):
    left, right = jnp.where(even, far, near), jnp.where(even, near, far)
    whole = jnp.concatenate([left, field_ref[slot].astype(F32), right], axis=1)
    half = LANES // 2
    tiles = [whole[:, i : i + LANES] for i in range(0, whole.shape[1], LANES)]
    low = lane_below(tiles[0].shape, half)
    tiles = [pltpu.roll(t, half, 1) for t in tiles]
    middle = jnp.concatenate([jnp.where(low, a, b) for a, b in zip(tiles, tiles[1:])], axis=1)
    height = middle.shape[0]
    row = lax.broadcasted_iota(jnp.int32, middle.shape, 0)
    above = jnp.where(row == 0, 0.0, pltpu.roll(middle, 1, 0))
    below = jnp.where(row == height - 1, 0.0, pltpu.roll(middle, height - 1, 0))
    return above, middle, below


def pair_weight(kernel_ref, slot):
    weight = kernel_ref[slot].astype(F32)
    span = weight.shape[1] // 3
    parts = [weight[:, a * span : (a + 1) * span] for a in range(3)]
    blank = jnp.zeros((weight.shape[0], LANES // 2), F32)
    first = jnp.concatenate([x for part in parts for x in (part, blank)], axis=1)
    second = jnp.concatenate([x for part in parts for x in (blank, part)], axis=1)
    return jnp.concatenate([first, second], axis=0).astype(BF16)


def prepare_kernel(edges_out, field, kernel, weight, upstream, *refs):
    field_ref, pair_ref, weight_ref, upstream_ref = refs[:4]
    field_edges, refs = refs[4 : 4 + edges_out[0]], refs[4 + edges_out[0] :]
    upstream_edges, row_edges = refs[: edges_out[0]], refs[edges_out[0] : -2]
    kernel_ref, sems = refs[-2:]
    depth = weight.shape[0]
    copies = [
        pltpu.make_async_copy(source, target, sems.at[i])
        for i, (source, target) in enumerate(
            (
                (field, field_ref),
                (upstream, upstream_ref),
                (kernel, kernel_ref),
                (weight, weight_ref.at[pl.ds(0, depth), :]),
            )
        )
    ]
    for copy in copies:
        copy.start()
    if weight_ref.shape[0] > depth:
        weight_ref[depth:, :] = jnp.zeros((weight_ref.shape[0] - depth, weight_ref.shape[1]), BF16)
    even = lax.rem(lax.axis_index("col"), 2) == 0
    reach = field_edges[0].shape[2]
    copies[0].wait()
    low, high = field_ref[:, :, :reach], field_ref[:, :, field_ref.shape[2] - reach :]
    for i, ref in enumerate(field_edges):
        ref[...] = jnp.where(even, low, high) if i else jnp.where(even, high, low)
    copies[1].wait()
    cells = upstream_ref[...].astype(F32)
    low, high = cells[:, 0, :], cells[:, cells.shape[1] - 1, :]
    for i, ref in enumerate(upstream_edges):
        ref[...] = (jnp.where(even, low, high) if i else jnp.where(even, high, low)).astype(BF16)
    even = lax.rem(lax.axis_index("tile"), 2) == 0
    low, high = upstream_ref[0], upstream_ref[upstream_ref.shape[0] - 1]
    for i, ref in enumerate(row_edges):
        ref[...] = jnp.where(even, low, high) if i else jnp.where(even, high, low)
    copies[2].wait()
    for slot in range(kernel_ref.shape[0]):
        pair_ref[slot] = pair_weight(kernel_ref, slot)
    copies[3].wait()


def slot_inputs(field_ref, kernel_ref, halo_refs, slot):
    even = lax.rem(lax.axis_index("col"), 2) == 0
    near = halo_refs[0][slot].astype(F32)
    far = halo_refs[1][slot].astype(F32) if len(halo_refs) > 1 else jnp.zeros_like(near)
    return window_rows(field_ref, near, far, even, slot), kernel_ref[slot]


def gate_of(shifted, weight):
    shifted = [s.astype(BF16) for s in shifted]
    pairs = shifted[0].shape[1] // LANES - 1
    lhs = jnp.concatenate(
        [
            jnp.concatenate([s[:, p * LANES : (p + 2) * LANES] for s in shifted], axis=1)
            for p in range(pairs)
        ],
        axis=0,
    )
    gate = lax.dot_general(lhs, weight, (((1,), (1,)), ((), ())), preferred_element_type=F32)
    return gate.reshape(pairs, -1, LANES)


def features_kernel(tiles, count_ref, field_ref, kernel_ref, weight_ref, *refs):
    halo_refs, out_refs, store = refs[: -tiles - 1], refs[-tiles - 1 : -1], refs[-1]
    slots, height, lanes = field_ref.shape
    pairs = lanes // LANES + 2
    main = ROWS * pairs
    col = lax.axis_index("col")

    def values(slot):
        shifted, weight = slot_inputs(field_ref, kernel_ref, halo_refs, slot)
        gate = gate_of(shifted, weight)
        value = gate / (1.0 + jnp.exp(-gate))
        live = slot < count_ref[0]
        first = jnp.where(live & (col > 0), value[:1], 0.0)
        last = jnp.where(live & (col < lax.axis_size("col") - 1), value[-1:], 0.0)
        return jnp.concatenate([first, jnp.where(live, value[1:-1], 0.0), last], axis=0)

    def around(bands, j):
        none = jnp.zeros_like(bands[0])
        sub = lax.broadcasted_iota(jnp.int32, none.shape, 1)
        both = jnp.where(sub >= 4, bands[j - 1] if j else none, bands[j + 1] if j + 1 < len(bands) else none)
        packed = [
            jnp.where(sub[0] < 4, pltpu.roll(both[q], 2, 0), pltpu.roll(both[q + 1], 6, 0))
            for q in range(0, pairs, 2)
        ]
        return jnp.concatenate(packed, axis=0)

    def put(both, lane_tile):
        here = slice(lane_tile * LANES, (lane_tile + 1) * LANES)
        bands = [[v[:, ROWS * j : ROWS * (j + 1)] for j in range(height // ROWS)] for v in both]
        for j in range(height // ROWS):
            for half in range(2):
                rows = bands[half][j].reshape(main, LANES)
                store[j, half * main : (half + 1) * main, here] = rows.astype(BF16)
            halo = jnp.concatenate([around(bands[half], j) for half in range(2)], axis=0)
            store[j, 2 * main :, here] = halo.astype(BF16)

    for slot in range(0, slots - 1, 2):
        put(interleave(values(slot), values(slot + 1)), slot // 2)
    if slots % 2:
        last = values(slots - 1)
        put(interleave(last, jnp.zeros_like(last)), slots // 2)
    for step, out in enumerate(out_refs):
        band = lax.bitwise_xor(lax.axis_index("tile"), step)
        out[...] = jnp.dot(store[band], weight_ref[...], preferred_element_type=F32).astype(BF16)


def backward_inputs_kernel(count_ref, field_ref, kernel_ref, *refs):
    halo_refs, (patch_ref, own_ref) = refs[:-2], refs[-2:]
    slots, height, lanes = field_ref.shape
    pairs = lanes // LANES
    bands = height // ROWS

    def by_band(value):
        return jnp.concatenate([value[:, ROWS * j : ROWS * (j + 1)] for j in range(bands)], axis=0)

    def values(slot):
        shifted, weight = slot_inputs(field_ref, kernel_ref, halo_refs, slot)
        gate = gate_of(shifted, weight)[1:-1]
        live = slot < count_ref[0]
        slope = by_band(jnp.where(live, silu_slope(gate), 0.0))
        patch_ref[slot, :, 6 * LANES :] = slope.reshape(-1, LANES).astype(BF16)
        for a, s in enumerate(shifted):
            patch = jnp.concatenate(
                [
                    s[ROWS * j : ROWS * (j + 1), p * LANES : (p + 2) * LANES]
                    for j in range(bands)
                    for p in range(1, pairs + 1)
                ],
                axis=0,
            )
            patch_ref[slot, :, 2 * a * LANES : 2 * (a + 1) * LANES] = patch.astype(BF16)
        return jnp.where(live, gate / (1.0 + jnp.exp(-gate)), 0.0)

    def put(even, odd, lane_tile):
        span = ROWS * pairs
        for j in range(bands):
            for half, value in enumerate((even, odd)):
                rows = value[:, ROWS * j : ROWS * (j + 1)].reshape(span, LANES)
                own_ref[
                    (2 * j + half) * span : (2 * j + half + 1) * span,
                    lane_tile * LANES : (lane_tile + 1) * LANES,
                ] = rows.astype(BF16)

    for slot in range(0, slots - 1, 2):
        put(*interleave(values(slot), values(slot + 1)), slot // 2)
    if slots % 2:
        last = values(slots - 1)
        put(*interleave(last, jnp.zeros_like(last)), slots // 2)


def upstream_kernel(main_ref, left_ref, right_ref, top_ref, bottom_ref, mix_ref, grad_ref, rows_ref):
    width = grad_ref.shape[0] - 2
    cells, hidden = main_ref.shape
    rows_ref[...] = jnp.zeros_like(rows_ref)
    places = (0, cells, cells + 16, cells + 32, cells + 32 + width)
    for place, ref in zip(places, (main_ref, left_ref, right_ref, top_ref, bottom_ref)):
        rows_ref[place : place + ref.shape[0], :] = ref[...]
    shape = ((width + 2) * 16, rows_ref.shape[0])
    target = lax.broadcasted_iota(jnp.int32, shape, 0)
    source = lax.broadcasted_iota(jnp.int32, shape, 1)
    column, row = lax.shift_right_logical(target, 4), target & 15
    want = (row - 1) * width + (column - 1)
    want = jnp.where(row == 0, places[3] + column - 1, want)
    want = jnp.where(row == ROWS + 1, places[4] + column - 1, want)
    want = jnp.where(column == 0, places[1] + row, want)
    want = jnp.where(column == width + 1, places[2] + row, want)
    want = jnp.where(row > ROWS + 1, -1, want)
    pick = jnp.where(source == want, 1.0, 0.0).astype(BF16)
    picked = jnp.dot(pick, rows_ref[...], preferred_element_type=F32).astype(BF16)
    grad = jnp.dot(picked, mix_ref[...], preferred_element_type=F32)
    grad_ref[...] = grad.reshape(width + 2, 16, hidden)


TAPS = [(a, b) for a in range(3) for b in range(3)]


def middle_kernel(tiles, grad_ref, depth_ref, *refs):
    term_refs, (act_grad_ref, hidden_ref, act, inner) = refs[:tiles], refs[tiles:]
    width, hidden = grad_ref.shape[0] - 2, grad_ref.shape[2]
    pairs = width // 2 + 2
    main = ROWS * pairs
    chunks = [(n, slice(n * LANES, (n + 1) * LANES)) for n in range(hidden // LANES)]
    for n, here in chunks:
        total = tree_sum([ref[:, here].astype(F32) for ref in term_refs]).astype(BF16).astype(F32)
        for p in range(pairs):
            for half in range(2):
                start = half * main + ROWS * p
                act[n, 2 * p + half, 2 : 2 + ROWS, :] = total[start : start + ROWS]
                start = 2 * main + half * main // 2 + 4 * p
                act[n, 2 * p + half, 0:2, :] = total[start : start + 2]
                act[n, 2 * p + half, 2 + ROWS : 4 + ROWS, :] = total[start + 2 : start + 4]

    def forward(column, carry):
        for n, here in chunks:
            terms = [
                depth_ref[3 * a + b : 3 * a + b + 1, here] * act[n, column + b, a : a + ROWS + 2, :] for a, b in TAPS
            ]
            before = tree_sum(terms)
            sig = 1.0 / (1.0 + jnp.exp(-before))
            slope = sig * (1.0 + before * (1.0 - sig))
            grad = grad_ref[column, 0 : ROWS + 2, here] * slope
            inner[n, column, 0 : ROWS + 2, :] = grad.astype(BF16).astype(F32)
            hidden_ref[column, :, here] = (before * sig)[1 : ROWS + 1]
        return carry

    lax.fori_loop(0, width + 2, forward, 0)

    def backward(column, carry):
        place = lax.shift_right_logical(column, 1) + (column & 1) * (width // 2)
        for n, here in chunks:
            terms = [
                depth_ref[3 * a + b : 3 * a + b + 1, here] * inner[n, column + 2 - b, 2 - a : 2 - a + ROWS, :]
                for a, b in TAPS
            ]
            act_grad_ref[place, :, here] = tree_sum(terms).astype(BF16)
        return carry

    lax.fori_loop(0, width, backward, 0)


def finish_kernel(hidden_ref, upstream_ref, mix_ref, act, inner, adjusted_ref, keep_ref, send_ref, held):
    chunks, columns = act.shape[:2]
    width = columns - 4
    cells, hidden = upstream_ref.shape
    target = lax.broadcasted_iota(jnp.int32, (cells, cells), 0)
    source = lax.broadcasted_iota(jnp.int32, (cells, cells), 1)
    pick = (source & (ROWS - 1)) * width + lax.shift_right_logical(source, 3) == target
    pick = jnp.where(pick, 1.0, 0.0).astype(BF16)
    by_column = hidden_ref[1 : width + 1].reshape(cells, hidden).astype(BF16)
    value = jnp.dot(pick, by_column, preferred_element_type=F32).astype(BF16)
    adjusted_ref[...] = lax.dot_general(
        value, mix_ref[...], (((1,), (1,)), ((), ())), preferred_element_type=F32
    ).astype(BF16)
    held[...] = lax.dot_general(
        upstream_ref[...], value, (((0,), (0,)), ((), ())), preferred_element_type=F32
    ).astype(BF16)

    def add(column, sums):
        new = []
        for n in range(chunks):
            own = inner[n, column + 1, 1 : 1 + ROWS, :]
            for t, (a, b) in enumerate(TAPS):
                new.append(sums[n * 9 + t] + act[n, column + 1 + b, 1 + a : 1 + a + ROWS, :] * own)
        return tuple(new)

    zero = jnp.zeros((ROWS, LANES), F32)
    sums = lax.fori_loop(0, width, add, (zero,) * (9 * chunks))
    rows = []
    for n in range(chunks):
        taps = [jnp.sum(sums[n * 9 + t], axis=0, keepdims=True) for t in range(9)]
        rows.append(jnp.concatenate(taps + [jnp.zeros((7, LANES), F32)], axis=0))
    depth = jnp.concatenate(rows, axis=1).astype(BF16)
    rep = lax.axis_index("rep")
    block = hidden // (lax.axis_size("tile") * lax.axis_size("col") * lax.axis_size("rep"))
    for ref, which in ((keep_ref, rep), (send_ref, 1 - rep)):
        for g in range((keep_ref.shape[0] - 16) // block):
            start = pl.multiple_of(2 * g * block + which * block, 16)
            ref[g * block : (g + 1) * block, :] = held[pl.ds(start, block), :]
        ref[keep_ref.shape[0] - 16 :, :] = depth


def spread_kernel(axis, block, count, *refs):
    in_refs, out_refs, held = refs[:count], refs[count:-1], refs[-1]
    held[...] = tree_sum([ref[...].astype(F32) for ref in in_refs]).astype(BF16)
    rows = out_refs[0].shape[0] - 16
    size = len(out_refs)
    for step, out in enumerate(out_refs):
        part = lax.bitwise_xor(lax.axis_index(axis), step)
        for g in range(rows // block):
            start = pl.multiple_of(g * size * block + part * block, 16)
            out[g * block : (g + 1) * block, :] = held[pl.ds(start, block), :]
        out[rows:, :] = held[held.shape[0] - 16 :, :]


def total_kernel(count, *refs):
    in_refs, (mix_ref, depth_ref) = refs[:count], refs[count:]
    total = tree_sum([ref[...].astype(F32) for ref in in_refs])
    rows = mix_ref.shape[0]
    mix_ref[...] = total[:rows]
    depth_ref[...] = total[rows : rows + depth_ref.shape[0]]


def in_gradient_kernel(tiles, own_ref, *refs):
    grad_refs, (keep, send, whole, held) = refs[:tiles], refs[tiles:]
    cells = grad_refs[0].shape[0]
    for step, ref in enumerate(grad_refs):
        start = pl.multiple_of(lax.bitwise_xor(lax.axis_index("tile"), step) * cells, 16)
        whole[pl.ds(start, cells), :] = ref[...]
    term = lax.dot_general(own_ref[...], whole[...], (((0,), (0,)), ((), ())), preferred_element_type=F32)
    half = keep.shape[0]
    rep = lax.axis_index("rep")
    held[...] = term[: 2 * half].astype(BF16)
    keep[...] = held[pl.ds(pl.multiple_of(rep * half, 16), half), :]
    send[...] = held[pl.ds(pl.multiple_of((1 - rep) * half, 16), half), :]


def group_gradient_kernel(tiles, rows_ref, weight_ref, patch_ref, group_keep, group_send, group_term):
    slots, lanes = patch_ref.shape[0], 6 * LANES
    channels = LANES // 2
    rows = rows_ref[...]
    cells = rows.shape[0] // tiles
    rep = lax.axis_index("rep")
    feature_grad = lax.dot_general(rows, weight_ref[...], (((1,), (1,)), ((), ())), preferred_element_type=F32)
    feature_grad = feature_grad.astype(BF16).astype(F32)
    blank = slots * channels % LANES
    if blank:
        feature_grad = jnp.concatenate(
            [feature_grad, jnp.zeros((feature_grad.shape[0], LANES - blank), F32)], axis=1
        )
    part = cells // 2

    def halves(value):
        return [
            jnp.concatenate(
                [value[cells * j + part * h : cells * j + part * (h + 1)] for j in range(tiles)], axis=0
            )
            for h in range(2)
        ]

    for slot in range(0, slots, 2):
        tile = feature_grad[:, slot * channels : slot * channels + LANES]
        both = interleave(*halves(tile))
        for k in range(slot, min(slot + 2, slots)):
            inner = (both[k - slot] * patch_ref[k, :, lanes:].astype(F32)).astype(BF16)
            term = lax.dot_general(inner, patch_ref[k, :, :lanes], (((0,), (0,)), ((), ())), preferred_element_type=F32)
            quarter = lanes // 3
            use = 3 * channels
            low = jnp.concatenate([term[:channels, quarter * a : quarter * a + use] for a in range(3)], axis=1)
            high = jnp.concatenate(
                [term[channels:, quarter * a + channels : quarter * (a + 1)] for a in range(3)], axis=1
            )
            group_term[channels * k : channels * (k + 1), :] = (low + high).astype(BF16)
    half = group_keep.shape[0]
    group_keep[...] = group_term[pl.ds(pl.multiple_of(rep * half, 16), half), :]
    group_send[...] = group_term[pl.ds(pl.multiple_of((1 - rep) * half, 16), half), :]


def call(kernel, outs, operands, scratch=(), flops=1 << 24, specs=None):
    shapes = [jax.ShapeDtypeStruct(s, d) for s, d in outs]
    moved = sum(o.size * o.dtype.itemsize for o in list(operands) + shapes)
    held = sum(math.prod(r.shape) * 4 for r in scratch if len(r.shape) > 1)
    return pl.pallas_call(
        kernel,
        out_shape=shapes,
        in_specs=specs or [SMEM if jnp.issubdtype(o.dtype, jnp.integer) else VMEM for o in operands],
        out_specs=[VMEM] * len(shapes),
        scratch_shapes=list(scratch),
        cost_estimate=pl.CostEstimate(flops=flops, bytes_accessed=moved, transcendentals=0),
        compiler_params=pltpu.CompilerParams(vmem_limit_bytes=(8 << 20) + 2 * (moved + held)),
    )(*operands)


def program(
    forcing,
    member_kernel_weight,
    member_counts,
    mixing_input_weight,
    depth_weight,
    mix_weight,
    cotangent,
):
    channels = member_kernel_weight.shape[2]
    slots = forcing.shape[1]
    height = forcing.shape[2]
    width = forcing.shape[3] // channels
    hidden = mixing_input_weight.shape[1]
    tiles, cols, reps = (lax.axis_size(a) for a in ("tile", "col", "rep"))
    pairs = width // 2 + 2
    cells = ROWS * width
    assert height == ROWS * tiles and 2 * channels == LANES and pairs % 2 == 0
    lane_tiles = -(-slots // 2)
    rows = hidden // (tiles * cols * reps)

    sides, ends = (1 if count == 2 else 2 for count in (cols, tiles))
    field, kernel, weight, upstream, *edges = call(
        functools.partial(prepare_kernel, (sides, ends)),
        [
            (forcing.shape[1:], BF16),
            ((slots, LANES, 6 * LANES), BF16),
            ((lane_tiles * LANES, hidden), BF16),
            (cotangent.shape[1:], BF16),
        ]
        + [((slots, height, 4 * channels), BF16)] * sides
        + [((ROWS, hidden), BF16)] * sides
        + [((width, hidden), BF16)] * ends,
        [
            pltpu.with_memory_space_constraint(x, pltpu.HBM)
            for x in (forcing[0], jnp.swapaxes(member_kernel_weight, 1, 2), mixing_input_weight, cotangent[0])
        ],
        [pltpu.VMEM((slots, channels, 9 * channels), BF16), pltpu.SemaphoreType.DMA((4,))],
        specs=[HBM] * 4,
    )
    halos = with_neighbours(edges[:sides], "col")
    top, bottom = in_order(with_neighbours(edges[2 * sides :], "tile"), "tile")
    sent = call(
        functools.partial(features_kernel, tiles),
        [((3 * ROWS * pairs, hidden), BF16)] * tiles,
        [member_counts, field, kernel, weight, *halos],
        [pltpu.VMEM((tiles, 3 * ROWS * pairs, lane_tiles * LANES), BF16)],
        flops=1 << 28,
    )
    terms = [swap(sent[step], "tile", step) if step else sent[0] for step in range(tiles)]

    even = lax.axis_index("col") % 2 == 0
    columns = []
    for i, edge in enumerate(edges[sides : 2 * sides]):
        last = even if i == 0 else ~even
        corners = [jnp.where(last, row[-1:], row[:1]) for row in (top, bottom)]
        columns.append(jnp.concatenate([corners[0], edge, corners[1]], axis=0))
    left, right = in_order(with_neighbours(columns, "col"), "col")
    flat_upstream = upstream.reshape(cells, hidden)
    (hidden_grad,) = call(
        upstream_kernel,
        [((width + 2, 16, hidden), F32)],
        [flat_upstream, left, right, top, bottom, mix_weight],
        [pltpu.VMEM((2 * LANES, hidden), BF16)],
        flops=1 << 28,
    )
    patch, own_features = call(
        backward_inputs_kernel,
        [
            ((slots, cells // 2 * tiles, 7 * LANES), BF16),
            ((cells * tiles, lane_tiles * LANES), BF16),
        ],
        [member_counts, field, kernel, *halos],
        flops=1 << 28,
    )

    act_grad, hidden_act, act, inner = call(
        functools.partial(middle_kernel, tiles),
        [
            ((width, ROWS, hidden), BF16),
            ((width + 2, ROWS, hidden), F32),
            ((hidden // LANES, width + 4, 16, LANES), F32),
            ((hidden // LANES, width + 2, 16, LANES), F32),
        ],
        [hidden_grad, depth_weight, *terms],
    )
    act_grad = act_grad.reshape(cells, hidden)
    grads = [swap(act_grad, "tile", step) if step else act_grad for step in range(tiles)]

    part = ((tiles * cols * rows + 16, hidden), BF16)
    adjusted, keep, send = call(
        finish_kernel,
        [((cells, hidden), BF16), part, part],
        [hidden_act, flat_upstream, mix_weight, act, inner],
        [pltpu.VMEM((hidden, hidden), BF16)],
    )
    arrived = [keep, swap(send, "rep", 1)]
    blocks = tiles * cols
    for axis in ("col", "tile"):
        size = lax.axis_size(axis)
        blocks //= size
        dealt = call(
            functools.partial(spread_kernel, axis, rows, len(arrived)),
            [((blocks * rows + 16, hidden), BF16)] * size,
            arrived,
            [pltpu.VMEM(arrived[0].shape, BF16)],
        )
        arrived = [swap(dealt[step], axis, step) if step else dealt[0] for step in range(size)]
    mix_grad, depth_grad = call(
        functools.partial(total_kernel, tiles), [((rows, hidden), F32), ((9, hidden), F32)], arrived
    )

    half = slots * channels // 2
    in_keep, in_send, whole = call(
        functools.partial(in_gradient_kernel, tiles),
        [((half, hidden), BF16), ((half, hidden), BF16), ((cells * tiles, hidden), BF16)],
        [own_features, *grads],
        [pltpu.VMEM((2 * half, hidden), BF16)],
    )
    group_keep, group_send = call(
        functools.partial(group_gradient_kernel, tiles),
        [((half, 9 * channels), BF16), ((half, 9 * channels), BF16)],
        [whole, mixing_input_weight, patch],
        [pltpu.VMEM((2 * half, 9 * channels), BF16)],
        flops=1 << 28,
    )
    in_grad = full_sum(in_keep, in_send).astype(F32)
    group_grad = full_sum(group_keep, group_send).reshape(slots, channels, -1)
    group_grad = jnp.swapaxes(group_grad, 1, 2).astype(F32)
    return (adjusted.reshape(cotangent.shape), mix_grad, depth_grad, in_grad, group_grad)


def solution(mesh):
    in_specs = (
        P(("groups", "rep"), "tile", None, "col"),
        P("tile", None, None),
        P("tile"),
        P("tile", None),
        P(),
        P(),
        P(("groups", "rep"), "tile", "col", None),
    )
    out_specs = (
        P(("groups", "rep"), "tile", "col", None),
        P(("groups", "tile", "col", "rep"), None),
        P("groups", None),
        P(("groups", "tile"), None),
        P(("groups", "tile"), None, None),
    )
    return jax.shard_map(program, mesh=mesh, in_specs=in_specs, out_specs=out_specs, check_vma=False)
```

```python
import functools
import math

import jax
import jax.numpy as jnp
from jax import lax
from jax.experimental import pallas as pl
from jax.experimental.pallas import tpu as pltpu
from jax.sharding import PartitionSpec as P


F32 = jnp.float32
BF16 = jnp.bfloat16
LANES = 128
ROWS = 8
VMEM = pl.BlockSpec(memory_space=pltpu.VMEM)
SMEM = pl.BlockSpec(memory_space=pltpu.SMEM)
HBM = pl.BlockSpec(memory_space=pltpu.HBM)


def swap(value, axis, step):
    return lax.ppermute(value, axis, [(i, i ^ step) for i in range(lax.axis_size(axis))])


def with_neighbours(values, axis):
    count = lax.axis_size(axis)
    received = []
    for first, value in enumerate(values):
        pairs = [(i, i + 1) for i in range(first, count - 1, 2)]
        received.append(lax.ppermute(value, axis, pairs + [(b, a) for a, b in pairs]))
    return received


def tree_sum(terms):
    while len(terms) > 1:
        terms = [a + b for a, b in zip(terms[::2], terms[1::2])] + terms[len(terms) & ~1 :]
    return terms[0]


def full_sum(keep, send):
    rows, lanes = keep.shape
    total = (keep.astype(F32) + swap(send, "rep", 1).astype(F32)).astype(BF16)
    step = 1
    while step < lax.axis_size("col"):
        total = (total.astype(F32) + swap(total, "col", step).astype(F32)).astype(BF16)
        step *= 2
    remote = swap(total, "rep", 1)
    (whole,) = call(join_kernel, [((2 * rows, lanes), F32)], [total, remote])
    return whole


def join_kernel(total_ref, remote_ref, out_ref):
    rows = total_ref.shape[0]
    rep = lax.axis_index("rep")
    out_ref[pl.ds(pl.multiple_of(rep * rows, 16), rows), :] = total_ref[...].astype(F32)
    out_ref[pl.ds(pl.multiple_of((1 - rep) * rows, 16), rows), :] = remote_ref[...].astype(F32)


def silu_slope(value):
    sig = 1.0 / (1.0 + jnp.exp(-value))
    return sig * (1.0 + value * (1.0 - sig))


def lane_below(shape, bound):
    return lax.broadcasted_iota(jnp.int32, shape, len(shape) - 1) < bound


def interleave(first, second):
    half = LANES // 2
    low = lane_below(first.shape, half)
    axis = first.ndim - 1
    return (
        jnp.where(low, first, pltpu.roll(second, half, axis)),
        jnp.where(low, pltpu.roll(first, half, axis), second),
    )


def window_rows(field_ref, halo_refs, slot, inner):
    even = lax.rem(lax.axis_index("col"), 2) == 0
    near = halo_refs[0][slot].astype(F32)
    far = halo_refs[1][slot].astype(F32) if len(halo_refs) > 1 else jnp.zeros_like(near)
    left, right = jnp.where(even, far, near), jnp.where(even, near, far)
    whole = jnp.concatenate([left, field_ref[slot].astype(F32), right], axis=1)
    half = LANES // 2
    tiles = [whole[:, i : i + LANES] for i in range(0, whole.shape[1], LANES)]
    low = lane_below(tiles[0].shape, half)
    tiles = [pltpu.roll(t, half, 1) for t in tiles]
    tiles = [jnp.where(low, a, b) for a, b in zip(tiles, tiles[1:])]
    if inner:
        tiles = tiles[1:-1]
    elif len(halo_refs) == 1:
        tiles = [jnp.where(even, b, a) for a, b in zip(tiles, tiles[1:])]
    middle = jnp.concatenate(tiles, axis=1)
    height = middle.shape[0]
    row = lax.broadcasted_iota(jnp.int32, middle.shape, 0)
    above = jnp.where(row == 0, 0.0, pltpu.roll(middle, 1, 0))
    below = jnp.where(row == height - 1, 0.0, pltpu.roll(middle, height - 1, 0))
    return above, middle, below


def pair_weight(kernel_ref, slot):
    weight = kernel_ref[slot].astype(F32)
    span = weight.shape[1] // 3
    parts = [weight[:, a * span : (a + 1) * span] for a in range(3)]
    blank = jnp.zeros((weight.shape[0], LANES // 2), F32)
    first = jnp.concatenate([x for part in parts for x in (part, blank)], axis=1)
    second = jnp.concatenate([x for part in parts for x in (blank, part)], axis=1)
    return jnp.concatenate([first, second], axis=0).astype(BF16)


def prepare_kernel(edges_out, field, kernel, weight, upstream, *refs):
    field_ref, pair_ref, weight_ref, upstream_ref = refs[:4]
    field_edges, refs = refs[4 : 4 + edges_out[0]], refs[4 + edges_out[0] :]
    upstream_edges, row_edges = refs[: edges_out[0]], refs[edges_out[0] : -2]
    kernel_ref, sems = refs[-2:]
    depth = weight.shape[0]
    copies = [
        pltpu.make_async_copy(source, target, sems.at[i])
        for i, (source, target) in enumerate(
            (
                (field, field_ref),
                (upstream, upstream_ref),
                (kernel, kernel_ref),
                (weight, weight_ref.at[pl.ds(0, depth), :]),
            )
        )
    ]
    for copy in copies:
        copy.start()
    if weight_ref.shape[0] > depth:
        weight_ref[depth:, :] = jnp.zeros((weight_ref.shape[0] - depth, weight_ref.shape[1]), BF16)
    even = lax.rem(lax.axis_index("col"), 2) == 0
    reach = field_edges[0].shape[2]
    copies[0].wait()
    low, high = field_ref[:, :, :reach], field_ref[:, :, field_ref.shape[2] - reach :]
    for i, ref in enumerate(field_edges):
        ref[...] = jnp.where(even, low, high) if i else jnp.where(even, high, low)
    copies[1].wait()
    cells = upstream_ref[...].astype(F32)
    low, high = cells[:, 0, :], cells[:, cells.shape[1] - 1, :]
    for i, ref in enumerate(upstream_edges):
        ref[...] = (jnp.where(even, low, high) if i else jnp.where(even, high, low)).astype(BF16)
    even = lax.rem(lax.axis_index("tile"), 2) == 0
    low, high = upstream_ref[0], upstream_ref[upstream_ref.shape[0] - 1]
    for i, ref in enumerate(row_edges):
        ref[...] = jnp.where(even, low, high) if i else jnp.where(even, high, low)
    copies[2].wait()
    for slot in range(kernel_ref.shape[0]):
        pair_ref[slot] = pair_weight(kernel_ref, slot)
    copies[3].wait()


def gate_of(shifted, weight):
    shifted = [s.astype(BF16) for s in shifted]
    pairs = shifted[0].shape[1] // LANES - 1
    lhs = jnp.concatenate(
        [
            jnp.concatenate([s[:, p * LANES : (p + 2) * LANES] for s in shifted], axis=1)
            for p in range(pairs)
        ],
        axis=0,
    )
    gate = lax.dot_general(lhs, weight, (((1,), (1,)), ((), ())), preferred_element_type=F32)
    return gate.reshape(pairs, -1, LANES)


def sent_pairs(width, cols):
    return width // 2 + (1 if cols == 2 else 2)


def features_kernel(tiles, pairs, count_ref, field_ref, kernel_ref, weight_ref, *refs):
    halo_refs, out_refs, store = refs[: -tiles - 1], refs[-tiles - 1 : -1], refs[-1]
    slots, height, _ = field_ref.shape
    main = ROWS * pairs
    col = lax.axis_index("col")

    def values(slot):
        gate = gate_of(window_rows(field_ref, halo_refs, slot, False), kernel_ref[slot])
        value = gate / (1.0 + jnp.exp(-gate))
        live = slot < count_ref[0]
        if len(halo_refs) == 1:
            return jnp.where(live, value, 0.0)
        first = jnp.where(live & (col > 0), value[:1], 0.0)
        last = jnp.where(live & (col < lax.axis_size("col") - 1), value[-1:], 0.0)
        return jnp.concatenate([first, jnp.where(live, value[1:-1], 0.0), last], axis=0)

    def put(both, lane_tile):
        here = slice(lane_tile * LANES, (lane_tile + 1) * LANES)
        bands = [[v[:, ROWS * j : ROWS * (j + 1)] for j in range(height // ROWS)] for v in both]
        none = jnp.zeros_like(bands[0][0])
        sub = lax.broadcasted_iota(jnp.int32, none.shape, 1)
        for j in range(height // ROWS):
            halo = []
            for half in range(2):
                rows = bands[half][j].reshape(main, LANES)
                store[j, half * main : (half + 1) * main, here] = rows.astype(BF16)
                above = bands[half][j - 1] if j else none
                below = bands[half][j + 1] if ROWS * (j + 1) < height else none
                halo.append(pltpu.roll(jnp.where(sub >= 4, above, below), 2 + 4 * half, 1))
            store[j, 2 * main :, here] = jnp.where(sub < 4, *halo).reshape(main, LANES).astype(BF16)

    for slot in range(0, slots - 1, 2):
        put(interleave(values(slot), values(slot + 1)), slot // 2)
    if slots % 2:
        last = values(slots - 1)
        put(interleave(last, jnp.zeros_like(last)), slots // 2)
    for step, out in enumerate(out_refs):
        band = lax.bitwise_xor(lax.axis_index("tile"), step)
        out[...] = jnp.dot(store[band], weight_ref[...], preferred_element_type=F32).astype(BF16)


def backward_inputs_kernel(count_ref, field_ref, kernel_ref, *refs):
    halo_refs, (patch_ref, own_ref) = refs[:-2], refs[-2:]
    slots, height, lanes = field_ref.shape
    pairs = lanes // LANES
    bands = height // ROWS

    def by_band(value):
        return jnp.concatenate([value[:, ROWS * j : ROWS * (j + 1)] for j in range(bands)], axis=0)

    def values(slot):
        shifted = window_rows(field_ref, halo_refs, slot, True)
        gate = gate_of(shifted, kernel_ref[slot])
        live = slot < count_ref[0]
        slope = by_band(jnp.where(live, silu_slope(gate), 0.0))
        patch_ref[slot, :, 6 * LANES :] = slope.reshape(-1, LANES).astype(BF16)
        for a, s in enumerate(shifted):
            patch = jnp.concatenate(
                [
                    s[ROWS * j : ROWS * (j + 1), p * LANES : (p + 2) * LANES]
                    for j in range(bands)
                    for p in range(pairs)
                ],
                axis=0,
            )
            patch_ref[slot, :, 2 * a * LANES : 2 * (a + 1) * LANES] = patch.astype(BF16)
        return jnp.where(live, gate / (1.0 + jnp.exp(-gate)), 0.0)

    def put(even, odd, lane_tile):
        span = ROWS * pairs
        for j in range(bands):
            for half, value in enumerate((even, odd)):
                rows = value[:, ROWS * j : ROWS * (j + 1)].reshape(span, LANES)
                own_ref[
                    (2 * j + half) * span : (2 * j + half + 1) * span,
                    lane_tile * LANES : (lane_tile + 1) * LANES,
                ] = rows.astype(BF16)

    for slot in range(0, slots - 1, 2):
        put(*interleave(values(slot), values(slot + 1)), slot // 2)
    if slots % 2:
        last = values(slots - 1)
        put(*interleave(last, jnp.zeros_like(last)), slots // 2)


def upstream_kernel(main_ref, top_ref, bottom_ref, mix_ref, *refs):
    column_refs, (grad_ref, rows_ref) = refs[:-2], refs[-2:]
    width = grad_ref.shape[0] - 2
    cells, hidden = main_ref.shape
    rows_ref[...] = jnp.zeros_like(rows_ref)
    even = lax.rem(lax.axis_index("col"), 2) == 0
    near = column_refs[0][...]
    far = column_refs[1][...] if len(column_refs) > 1 else jnp.zeros_like(near)
    places = (0, cells, cells + 16, cells + 32, cells + 32 + width)
    values = (main_ref[...], jnp.where(even, far, near), jnp.where(even, near, far), top_ref[...], bottom_ref[...])
    for place, value in zip(places, values):
        rows_ref[place : place + value.shape[0], :] = value
    shape = ((width + 2) * 16, rows_ref.shape[0])
    target = lax.broadcasted_iota(jnp.int32, shape, 0)
    source = lax.broadcasted_iota(jnp.int32, shape, 1)
    column, row = lax.shift_right_logical(target, 4), target & 15
    want = (row - 1) * width + (column - 1)
    want = jnp.where(row == 0, places[3] + column - 1, want)
    want = jnp.where(row == ROWS + 1, places[4] + column - 1, want)
    want = jnp.where(column == 0, places[1] + row, want)
    want = jnp.where(column == width + 1, places[2] + row, want)
    want = jnp.where(row > ROWS + 1, -1, want)
    pick = jnp.where(source == want, 1.0, 0.0).astype(BF16)
    picked = jnp.dot(pick, rows_ref[...], preferred_element_type=F32).astype(BF16)
    grad = jnp.dot(picked, mix_ref[...], preferred_element_type=F32)
    grad_ref[...] = grad.reshape(width + 2, 16, hidden)


TAPS = [(a, b) for a in range(3) for b in range(3)]


def middle_kernel(tiles, grad_ref, depth_ref, *refs):
    term_refs, (act_grad_ref, hidden_ref, act, inner) = refs[:tiles], refs[tiles:]
    width, hidden = grad_ref.shape[0] - 2, grad_ref.shape[2]
    cols = lax.axis_size("col")
    pairs = sent_pairs(width, cols)
    main = ROWS * pairs
    before_block = jnp.where(lax.axis_index("col") == 0, 2, 0) if cols == 2 else 0
    chunks = [(n, slice(n * LANES, (n + 1) * LANES)) for n in range(hidden // LANES)]
    for n, here in chunks:
        total = tree_sum([ref[:, here].astype(F32) for ref in term_refs]).astype(BF16).astype(F32)
        for p in range(pairs):
            for half in range(2):
                column = before_block + 2 * p + half
                start = half * main + ROWS * p
                act[n, column, 2 : 2 + ROWS, :] = total[start : start + ROWS]
                start = 2 * main + ROWS * p + 4 * half
                act[n, column, 0:2, :] = total[start : start + 2]
                act[n, column, 2 + ROWS : 4 + ROWS, :] = total[start + 2 : start + 4]
        if cols == 2:
            for half in range(2):
                act[n, lax.rem(before_block + width + 2, width + 4) + half] = jnp.zeros(act.shape[2:], F32)

    def forward(column, carry):
        for n, here in chunks:
            terms = [
                depth_ref[3 * a + b : 3 * a + b + 1, here] * act[n, column + b, a : a + ROWS + 2, :] for a, b in TAPS
            ]
            before = tree_sum(terms)
            sig = 1.0 / (1.0 + jnp.exp(-before))
            slope = sig * (1.0 + before * (1.0 - sig))
            grad = grad_ref[column, 0 : ROWS + 2, here] * slope
            inner[n, column, 0 : ROWS + 2, :] = grad.astype(BF16).astype(F32)
            hidden_ref[column, :, here] = (before * sig)[1 : ROWS + 1]
        return carry

    lax.fori_loop(0, width + 2, forward, 0)

    def backward(column, carry):
        place = lax.shift_right_logical(column, 1) + (column & 1) * (width // 2)
        for n, here in chunks:
            terms = [
                depth_ref[3 * a + b : 3 * a + b + 1, here] * inner[n, column + 2 - b, 2 - a : 2 - a + ROWS, :]
                for a, b in TAPS
            ]
            act_grad_ref[place, :, here] = tree_sum(terms).astype(BF16)
        return carry

    lax.fori_loop(0, width, backward, 0)


def finish_kernel(hidden_ref, upstream_ref, mix_ref, act, inner, adjusted_ref, keep_ref, send_ref, held):
    chunks, columns = act.shape[:2]
    width = columns - 4
    cells, hidden = upstream_ref.shape
    target = lax.broadcasted_iota(jnp.int32, (cells, cells), 0)
    source = lax.broadcasted_iota(jnp.int32, (cells, cells), 1)
    pick = (source & (ROWS - 1)) * width + lax.shift_right_logical(source, 3) == target
    pick = jnp.where(pick, 1.0, 0.0).astype(BF16)
    by_column = hidden_ref[1 : width + 1].reshape(cells, hidden).astype(BF16)
    value = jnp.dot(pick, by_column, preferred_element_type=F32).astype(BF16)
    adjusted_ref[...] = lax.dot_general(
        value, mix_ref[...], (((1,), (1,)), ((), ())), preferred_element_type=F32
    ).astype(BF16)
    held[...] = lax.dot_general(
        upstream_ref[...], value, (((0,), (0,)), ((), ())), preferred_element_type=F32
    ).astype(BF16)

    def add(column, sums):
        new = []
        for n in range(chunks):
            own = inner[n, column + 1, 1 : 1 + ROWS, :]
            for t, (a, b) in enumerate(TAPS):
                new.append(sums[n * 9 + t] + act[n, column + 1 + b, 1 + a : 1 + a + ROWS, :] * own)
        return tuple(new)

    zero = jnp.zeros((ROWS, LANES), F32)
    sums = lax.fori_loop(0, width, add, (zero,) * (9 * chunks))
    rows = []
    for n in range(chunks):
        taps = [jnp.sum(sums[n * 9 + t], axis=0, keepdims=True) for t in range(9)]
        rows.append(jnp.concatenate(taps + [jnp.zeros((7, LANES), F32)], axis=0))
    depth = jnp.concatenate(rows, axis=1).astype(BF16)
    rep = lax.axis_index("rep")
    block = hidden // (lax.axis_size("tile") * lax.axis_size("col") * lax.axis_size("rep"))
    for ref, which in ((keep_ref, rep), (send_ref, 1 - rep)):
        for g in range((keep_ref.shape[0] - 16) // block):
            start = pl.multiple_of(2 * g * block + which * block, 16)
            ref[g * block : (g + 1) * block, :] = held[pl.ds(start, block), :]
        ref[keep_ref.shape[0] - 16 :, :] = depth


def spread_kernel(axis, block, count, *refs):
    in_refs, out_refs, held = refs[:count], refs[count:-1], refs[-1]
    held[...] = tree_sum([ref[...].astype(F32) for ref in in_refs]).astype(BF16)
    rows = out_refs[0].shape[0] - 16
    size = len(out_refs)
    for step, out in enumerate(out_refs):
        part = lax.bitwise_xor(lax.axis_index(axis), step)
        for g in range(rows // block):
            start = pl.multiple_of(g * size * block + part * block, 16)
            out[g * block : (g + 1) * block, :] = held[pl.ds(start, block), :]
        out[rows:, :] = held[held.shape[0] - 16 :, :]


def total_kernel(count, *refs):
    in_refs, (mix_ref, depth_ref) = refs[:count], refs[count:]
    total = tree_sum([ref[...].astype(F32) for ref in in_refs])
    rows = mix_ref.shape[0]
    mix_ref[...] = total[:rows]
    depth_ref[...] = total[rows : rows + depth_ref.shape[0]]


def corner_kernel(ends, sides, *refs):
    row_refs, edge_refs, (top_ref, bottom_ref), out_refs = (
        refs[:ends],
        refs[ends : ends + sides],
        refs[ends + sides : ends + sides + 2],
        refs[ends + sides + 2 :],
    )
    even = lax.rem(lax.axis_index("tile"), 2) == 0
    near = row_refs[0][...].astype(F32)
    far = row_refs[1][...].astype(F32) if ends > 1 else jnp.zeros_like(near)
    top, bottom = jnp.where(even, far, near), jnp.where(even, near, far)
    top_ref[...] = top.astype(BF16)
    bottom_ref[...] = bottom.astype(BF16)
    last = lax.rem(lax.axis_index("col"), 2) == 0
    for i, (edge, out) in enumerate(zip(edge_refs, out_refs)):
        pick = last if i == 0 else ~last
        ends_of = [jnp.where(pick, row[-1:], row[:1]) for row in (top, bottom)]
        blank = jnp.zeros((16 - ROWS - 2, top.shape[1]), F32)
        out[...] = jnp.concatenate([ends_of[0], edge[...].astype(F32), ends_of[1], blank], axis=0).astype(BF16)


def in_gradient_kernel(tiles, own_ref, *refs):
    grad_refs, (keep, send, whole, held) = refs[:tiles], refs[tiles:]
    cells = grad_refs[0].shape[0]
    for step, ref in enumerate(grad_refs):
        start = pl.multiple_of(lax.bitwise_xor(lax.axis_index("tile"), step) * cells, 16)
        whole[pl.ds(start, cells), :] = ref[...]
    term = lax.dot_general(own_ref[...], whole[...], (((0,), (0,)), ((), ())), preferred_element_type=F32)
    half = keep.shape[0]
    rep = lax.axis_index("rep")
    held[...] = term[: 2 * half].astype(BF16)
    keep[...] = held[pl.ds(pl.multiple_of(rep * half, 16), half), :]
    send[...] = held[pl.ds(pl.multiple_of((1 - rep) * half, 16), half), :]


def group_gradient_kernel(tiles, rows_ref, weight_ref, patch_ref, group_keep, group_send, group_term):
    slots, lanes = patch_ref.shape[0], 6 * LANES
    channels = LANES // 2
    rows = rows_ref[...]
    cells = rows.shape[0] // tiles
    rep = lax.axis_index("rep")
    feature_grad = lax.dot_general(rows, weight_ref[...], (((1,), (1,)), ((), ())), preferred_element_type=F32)
    feature_grad = feature_grad.astype(BF16).astype(F32)
    blank = slots * channels % LANES
    if blank:
        feature_grad = jnp.concatenate(
            [feature_grad, jnp.zeros((feature_grad.shape[0], LANES - blank), F32)], axis=1
        )
    part = cells // 2

    def halves(value):
        return [
            jnp.concatenate(
                [value[cells * j + part * h : cells * j + part * (h + 1)] for j in range(tiles)], axis=0
            )
            for h in range(2)
        ]

    for slot in range(0, slots, 2):
        tile = feature_grad[:, slot * channels : slot * channels + LANES]
        both = interleave(*halves(tile))
        for k in range(slot, min(slot + 2, slots)):
            inner = (both[k - slot] * patch_ref[k, :, lanes:].astype(F32)).astype(BF16)
            term = lax.dot_general(inner, patch_ref[k, :, :lanes], (((0,), (0,)), ((), ())), preferred_element_type=F32)
            quarter = lanes // 3
            use = 3 * channels
            low = jnp.concatenate([term[:channels, quarter * a : quarter * a + use] for a in range(3)], axis=1)
            high = jnp.concatenate(
                [term[channels:, quarter * a + channels : quarter * (a + 1)] for a in range(3)], axis=1
            )
            group_term[channels * k : channels * (k + 1), :] = (low + high).astype(BF16)
    half = group_keep.shape[0]
    group_keep[...] = group_term[pl.ds(pl.multiple_of(rep * half, 16), half), :]
    group_send[...] = group_term[pl.ds(pl.multiple_of((1 - rep) * half, 16), half), :]


def call(kernel, outs, operands, scratch=(), flops=1 << 24, specs=None):
    shapes = [jax.ShapeDtypeStruct(s, d) for s, d in outs]
    moved = sum(o.size * o.dtype.itemsize for o in list(operands) + shapes)
    held = sum(math.prod(r.shape) * 4 for r in scratch if len(r.shape) > 1)
    return pl.pallas_call(
        kernel,
        out_shape=shapes,
        in_specs=specs or [SMEM if jnp.issubdtype(o.dtype, jnp.integer) else VMEM for o in operands],
        out_specs=[VMEM] * len(shapes),
        scratch_shapes=list(scratch),
        cost_estimate=pl.CostEstimate(flops=flops, bytes_accessed=moved, transcendentals=0),
        compiler_params=pltpu.CompilerParams(vmem_limit_bytes=(8 << 20) + 2 * (moved + held)),
    )(*operands)


def program(
    forcing,
    member_kernel_weight,
    member_counts,
    mixing_input_weight,
    depth_weight,
    mix_weight,
    cotangent,
):
    channels = member_kernel_weight.shape[2]
    slots = forcing.shape[1]
    height = forcing.shape[2]
    width = forcing.shape[3] // channels
    hidden = mixing_input_weight.shape[1]
    tiles, cols, reps = (lax.axis_size(a) for a in ("tile", "col", "rep"))
    pairs = sent_pairs(width, cols)
    cells = ROWS * width
    assert height == ROWS * tiles and 2 * channels == LANES
    lane_tiles = -(-slots // 2)
    rows = hidden // (tiles * cols * reps)

    sides, ends = (1 if count == 2 else 2 for count in (cols, tiles))
    field, kernel, weight, upstream, *edges = call(
        functools.partial(prepare_kernel, (sides, ends)),
        [
            (forcing.shape[1:], BF16),
            ((slots, LANES, 6 * LANES), BF16),
            ((lane_tiles * LANES, hidden), BF16),
            (cotangent.shape[1:], BF16),
        ]
        + [((slots, height, 4 * channels), BF16)] * sides
        + [((ROWS, hidden), BF16)] * sides
        + [((width, hidden), BF16)] * ends,
        [
            pltpu.with_memory_space_constraint(x, pltpu.HBM)
            for x in (forcing[0], jnp.swapaxes(member_kernel_weight, 1, 2), mixing_input_weight, cotangent[0])
        ],
        [pltpu.VMEM((slots, channels, 9 * channels), BF16), pltpu.SemaphoreType.DMA((4,))],
        specs=[HBM] * 4,
    )
    halos = with_neighbours(edges[:sides], "col")
    rows_near = with_neighbours(edges[2 * sides :], "tile")
    sent = call(
        functools.partial(features_kernel, tiles, pairs),
        [((3 * ROWS * pairs, hidden), BF16)] * tiles,
        [member_counts, field, kernel, weight, *halos],
        [pltpu.VMEM((tiles, 3 * ROWS * pairs, lane_tiles * LANES), BF16)],
        flops=1 << 28,
    )
    terms = [swap(sent[step], "tile", step) if step else sent[0] for step in range(tiles)]

    top, bottom, *columns = call(
        functools.partial(corner_kernel, ends, sides),
        [((width, hidden), BF16)] * 2 + [((16, hidden), BF16)] * sides,
        [*rows_near, *edges[sides : 2 * sides]],
    )
    columns = with_neighbours(columns, "col")
    flat_upstream = upstream.reshape(cells, hidden)
    (hidden_grad,) = call(
        upstream_kernel,
        [((width + 2, 16, hidden), F32)],
        [flat_upstream, top, bottom, mix_weight, *columns],
        [pltpu.VMEM((2 * LANES, hidden), BF16)],
        flops=1 << 28,
    )
    patch, own_features = call(
        backward_inputs_kernel,
        [
            ((slots, cells // 2 * tiles, 7 * LANES), BF16),
            ((cells * tiles, lane_tiles * LANES), BF16),
        ],
        [member_counts, field, kernel, *halos],
        flops=1 << 28,
    )

    act_grad, hidden_act, act, inner = call(
        functools.partial(middle_kernel, tiles),
        [
            ((width, ROWS, hidden), BF16),
            ((width + 2, ROWS, hidden), F32),
            ((hidden // LANES, width + 4, 16, LANES), F32),
            ((hidden // LANES, width + 2, 16, LANES), F32),
        ],
        [hidden_grad, depth_weight, *terms],
    )
    act_grad = act_grad.reshape(cells, hidden)
    grads = [swap(act_grad, "tile", step) if step else act_grad for step in range(tiles)]

    part = ((tiles * cols * rows + 16, hidden), BF16)
    adjusted, keep, send = call(
        finish_kernel,
        [((cells, hidden), BF16), part, part],
        [hidden_act, flat_upstream, mix_weight, act, inner],
        [pltpu.VMEM((hidden, hidden), BF16)],
    )
    arrived = [keep, swap(send, "rep", 1)]
    blocks = tiles * cols
    for axis in ("col", "tile"):
        size = lax.axis_size(axis)
        blocks //= size
        dealt = call(
            functools.partial(spread_kernel, axis, rows, len(arrived)),
            [((blocks * rows + 16, hidden), BF16)] * size,
            arrived,
            [pltpu.VMEM(arrived[0].shape, BF16)],
        )
        arrived = [swap(dealt[step], axis, step) if step else dealt[0] for step in range(size)]
    mix_grad, depth_grad = call(
        functools.partial(total_kernel, tiles), [((rows, hidden), F32), ((9, hidden), F32)], arrived
    )

    half = slots * channels // 2
    in_keep, in_send, whole = call(
        functools.partial(in_gradient_kernel, tiles),
        [((half, hidden), BF16), ((half, hidden), BF16), ((cells * tiles, hidden), BF16)],
        [own_features, *grads],
        [pltpu.VMEM((2 * half, hidden), BF16)],
    )
    group_keep, group_send = call(
        functools.partial(group_gradient_kernel, tiles),
        [((half, 9 * channels), BF16), ((half, 9 * channels), BF16)],
        [whole, mixing_input_weight, patch],
        [pltpu.VMEM((2 * half, 9 * channels), BF16)],
        flops=1 << 28,
    )
    in_grad = full_sum(in_keep, in_send)
    group_grad = full_sum(group_keep, group_send).reshape(slots, channels, -1)
    group_grad = jnp.swapaxes(group_grad, 1, 2)
    return (adjusted.reshape(cotangent.shape), mix_grad, depth_grad, in_grad, group_grad)


def solution(mesh):
    in_specs = (
        P(("groups", "rep"), "tile", None, "col"),
        P("tile", None, None),
        P("tile"),
        P("tile", None),
        P(),
        P(),
        P(("groups", "rep"), "tile", "col", None),
    )
    out_specs = (
        P(("groups", "rep"), "tile", "col", None),
        P(("groups", "tile", "col", "rep"), None),
        P("groups", None),
        P(("groups", "tile"), None),
        P(("groups", "tile"), None, None),
    )
    return jax.shard_map(program, mesh=mesh, in_specs=in_specs, out_specs=out_specs, check_vma=False)
```

```python
import functools
import math

import jax
import jax.numpy as jnp
from jax import lax
from jax.experimental import pallas as pl
from jax.experimental.pallas import tpu as pltpu
from jax.sharding import PartitionSpec as P


F32 = jnp.float32
BF16 = jnp.bfloat16
LANES = 128
ROWS = 8
VMEM = pl.BlockSpec(memory_space=pltpu.VMEM)
SMEM = pl.BlockSpec(memory_space=pltpu.SMEM)
HBM = pl.BlockSpec(memory_space=pltpu.HBM)


def swap(value, axis, step):
    return lax.ppermute(value, axis, [(i, i ^ step) for i in range(lax.axis_size(axis))])


def with_neighbours(values, axis):
    count = lax.axis_size(axis)
    received = []
    for first, value in enumerate(values):
        pairs = [(i, i + 1) for i in range(first, count - 1, 2)]
        received.append(lax.ppermute(value, axis, pairs + [(b, a) for a, b in pairs]))
    return received


def tree_sum(terms):
    while len(terms) > 1:
        terms = [a + b for a, b in zip(terms[::2], terms[1::2])] + terms[len(terms) & ~1 :]
    return terms[0]


def full_sum(keep, send):
    total = (keep.astype(F32) + swap(send, "rep", 1).astype(F32)).astype(BF16)
    step = 1
    while step < lax.axis_size("col"):
        total = (total.astype(F32) + swap(total, "col", step).astype(F32)).astype(BF16)
        step *= 2
    remote = swap(total, "rep", 1)
    return total, remote


def join_kernel(parts, *refs):
    in_refs, (in_out, group_out) = refs[:-2], refs[-2:]
    rows = in_refs[0].shape[0]
    rep = lax.axis_index("rep")
    for i in range(parts):
        for ref, which in ((in_refs[2 * i], rep), (in_refs[2 * i + 1], 1 - rep)):
            here = pl.ds(pl.multiple_of(which * rows, 16), rows)
            wide = in_refs[0].shape[1] if i < parts - 1 else in_out.shape[1] - i * in_refs[0].shape[1]
            at = in_out.shape[1] - wide if i == parts - 1 else i * wide
            in_out[here, at : at + wide] = ref[:, :wide].astype(F32)
            if i == parts - 1:
                group_out[here, :] = ref[:, wide : wide + group_out.shape[1]].astype(F32)


def silu_slope(value):
    sig = 1.0 / (1.0 + jnp.exp(-value))
    return sig * (1.0 + value * (1.0 - sig))


def lane_below(shape, bound):
    return lax.broadcasted_iota(jnp.int32, shape, len(shape) - 1) < bound


def interleave(first, second):
    half = LANES // 2
    low = lane_below(first.shape, half)
    axis = first.ndim - 1
    return (
        jnp.where(low, first, pltpu.roll(second, half, axis)),
        jnp.where(low, pltpu.roll(first, half, axis), second),
    )


def window_rows(field_ref, halo_refs, slot, inner):
    even = lax.rem(lax.axis_index("col"), 2) == 0
    near = halo_refs[0][slot].astype(F32)
    far = halo_refs[1][slot].astype(F32) if len(halo_refs) > 1 else jnp.zeros_like(near)
    left, right = jnp.where(even, far, near), jnp.where(even, near, far)
    whole = jnp.concatenate([left, field_ref[slot].astype(F32), right], axis=1)
    half = LANES // 2
    tiles = [whole[:, i : i + LANES] for i in range(0, whole.shape[1], LANES)]
    low = lane_below(tiles[0].shape, half)
    tiles = [pltpu.roll(t, half, 1) for t in tiles]
    tiles = [jnp.where(low, a, b) for a, b in zip(tiles, tiles[1:])]
    if inner:
        tiles = tiles[1:-1]
    elif len(halo_refs) == 1:
        tiles = [jnp.where(even, b, a) for a, b in zip(tiles, tiles[1:])]
    middle = jnp.concatenate(tiles, axis=1)
    height = middle.shape[0]
    row = lax.broadcasted_iota(jnp.int32, middle.shape, 0)
    above = jnp.where(row == 0, 0.0, pltpu.roll(middle, 1, 0))
    below = jnp.where(row == height - 1, 0.0, pltpu.roll(middle, height - 1, 0))
    return above, middle, below


def pair_weight(kernel_ref, slot):
    weight = kernel_ref[slot].astype(F32)
    span = weight.shape[1] // 3
    parts = [weight[:, a * span : (a + 1) * span] for a in range(3)]
    blank = jnp.zeros((weight.shape[0], LANES // 2), F32)
    first = jnp.concatenate([x for part in parts for x in (part, blank)], axis=1)
    second = jnp.concatenate([x for part in parts for x in (blank, part)], axis=1)
    return jnp.concatenate([first, second], axis=0).astype(BF16)


def prepare_kernel(edges_out, field, kernel, weight, upstream, *refs):
    field_ref, pair_ref, weight_ref, upstream_ref = refs[:4]
    field_edges, refs = refs[4 : 4 + edges_out[0]], refs[4 + edges_out[0] :]
    upstream_edges, row_edges = refs[: edges_out[0]], refs[edges_out[0] : -2]
    kernel_ref, sems = refs[-2:]
    depth = weight.shape[0]
    copies = [
        pltpu.make_async_copy(source, target, sems.at[i])
        for i, (source, target) in enumerate(
            (
                (field, field_ref),
                (upstream, upstream_ref),
                (kernel, kernel_ref),
                (weight, weight_ref.at[pl.ds(0, depth), :]),
            )
        )
    ]
    for copy in copies:
        copy.start()
    if weight_ref.shape[0] > depth:
        weight_ref[depth:, :] = jnp.zeros((weight_ref.shape[0] - depth, weight_ref.shape[1]), BF16)
    even = lax.rem(lax.axis_index("col"), 2) == 0
    reach = field_edges[0].shape[2]
    copies[0].wait()
    low, high = field_ref[:, :, :reach], field_ref[:, :, field_ref.shape[2] - reach :]
    for i, ref in enumerate(field_edges):
        ref[...] = jnp.where(even, low, high) if i else jnp.where(even, high, low)
    copies[1].wait()
    cells = upstream_ref[...].astype(F32)
    low, high = cells[:, 0, :], cells[:, cells.shape[1] - 1, :]
    for i, ref in enumerate(upstream_edges):
        ref[...] = (jnp.where(even, low, high) if i else jnp.where(even, high, low)).astype(BF16)
    even = lax.rem(lax.axis_index("tile"), 2) == 0
    low, high = upstream_ref[0], upstream_ref[upstream_ref.shape[0] - 1]
    for i, ref in enumerate(row_edges):
        ref[...] = jnp.where(even, low, high) if i else jnp.where(even, high, low)
    copies[2].wait()
    for slot in range(kernel_ref.shape[0]):
        pair_ref[slot] = pair_weight(kernel_ref, slot)
    copies[3].wait()


def gate_of(shifted, weight):
    shifted = [s.astype(BF16) for s in shifted]
    pairs = shifted[0].shape[1] // LANES - 1
    lhs = jnp.concatenate(
        [
            jnp.concatenate([s[:, p * LANES : (p + 2) * LANES] for s in shifted], axis=1)
            for p in range(pairs)
        ],
        axis=0,
    )
    gate = lax.dot_general(lhs, weight, (((1,), (1,)), ((), ())), preferred_element_type=F32)
    return gate.reshape(pairs, -1, LANES)


def sent_pairs(width, cols):
    return width // 2 + (1 if cols == 2 else 2)


def features_kernel(tiles, pairs, parts, count_ref, field_ref, kernel_ref, weight_ref, *refs):
    outs = tiles * parts
    halo_refs, out_refs, store = refs[: -outs - 1], refs[-outs - 1 : -1], refs[-1]
    slots, height, _ = field_ref.shape
    main = ROWS * pairs
    col = lax.axis_index("col")

    def values(slot):
        gate = gate_of(window_rows(field_ref, halo_refs, slot, False), kernel_ref[slot])
        value = gate / (1.0 + jnp.exp(-gate))
        live = slot < count_ref[0]
        if len(halo_refs) == 1:
            return jnp.where(live, value, 0.0)
        first = jnp.where(live & (col > 0), value[:1], 0.0)
        last = jnp.where(live & (col < lax.axis_size("col") - 1), value[-1:], 0.0)
        return jnp.concatenate([first, jnp.where(live, value[1:-1], 0.0), last], axis=0)

    def put(both, lane_tile):
        here = slice(lane_tile * LANES, (lane_tile + 1) * LANES)
        bands = [[v[:, ROWS * j : ROWS * (j + 1)] for j in range(height // ROWS)] for v in both]
        none = jnp.zeros_like(bands[0][0])
        sub = lax.broadcasted_iota(jnp.int32, none.shape, 1)
        for j in range(height // ROWS):
            halo = []
            for half in range(2):
                rows = bands[half][j].reshape(main, LANES)
                store[j, half * main : (half + 1) * main, here] = rows.astype(BF16)
                above = bands[half][j - 1] if j else none
                below = bands[half][j + 1] if ROWS * (j + 1) < height else none
                halo.append(pltpu.roll(jnp.where(sub >= 4, above, below), 2 + 4 * half, 1))
            store[j, 2 * main :, here] = jnp.where(sub < 4, *halo).reshape(main, LANES).astype(BF16)

    for slot in range(0, slots - 1, 2):
        put(interleave(values(slot), values(slot + 1)), slot // 2)
    if slots % 2:
        last = values(slots - 1)
        put(interleave(last, jnp.zeros_like(last)), slots // 2)
    for step in range(tiles):
        band = lax.bitwise_xor(lax.axis_index("tile"), step)
        term = jnp.dot(store[band], weight_ref[...], preferred_element_type=F32).astype(BF16)
        for part in range(parts):
            out = out_refs[part * tiles + step]
            out[...] = term[:, part * out.shape[1] : (part + 1) * out.shape[1]]


def backward_inputs_kernel(count_ref, field_ref, kernel_ref, *refs):
    halo_refs, (patch_ref, own_ref) = refs[:-2], refs[-2:]
    slots, height, lanes = field_ref.shape
    pairs = lanes // LANES
    bands = height // ROWS

    def by_band(value):
        return jnp.concatenate([value[:, ROWS * j : ROWS * (j + 1)] for j in range(bands)], axis=0)

    def values(slot):
        shifted = window_rows(field_ref, halo_refs, slot, True)
        gate = gate_of(shifted, kernel_ref[slot])
        live = slot < count_ref[0]
        slope = by_band(jnp.where(live, silu_slope(gate), 0.0))
        patch_ref[slot, :, 6 * LANES :] = slope.reshape(-1, LANES).astype(BF16)
        for a, s in enumerate(shifted):
            patch = jnp.concatenate(
                [
                    s[ROWS * j : ROWS * (j + 1), p * LANES : (p + 2) * LANES]
                    for j in range(bands)
                    for p in range(pairs)
                ],
                axis=0,
            )
            patch_ref[slot, :, 2 * a * LANES : 2 * (a + 1) * LANES] = patch.astype(BF16)
        return jnp.where(live, gate / (1.0 + jnp.exp(-gate)), 0.0)

    def put(even, odd, lane_tile):
        span = ROWS * pairs
        for j in range(bands):
            for half, value in enumerate((even, odd)):
                rows = value[:, ROWS * j : ROWS * (j + 1)].reshape(span, LANES)
                own_ref[
                    (2 * j + half) * span : (2 * j + half + 1) * span,
                    lane_tile * LANES : (lane_tile + 1) * LANES,
                ] = rows.astype(BF16)

    for slot in range(0, slots - 1, 2):
        put(*interleave(values(slot), values(slot + 1)), slot // 2)
    if slots % 2:
        last = values(slots - 1)
        put(*interleave(last, jnp.zeros_like(last)), slots // 2)


def upstream_kernel(main_ref, top_ref, bottom_ref, mix_ref, *refs):
    column_refs, (grad_ref, rows_ref) = refs[:-2], refs[-2:]
    width = grad_ref.shape[0] - 2
    cells, hidden = main_ref.shape
    rows_ref[...] = jnp.zeros_like(rows_ref)
    even = lax.rem(lax.axis_index("col"), 2) == 0
    near = column_refs[0][...]
    far = column_refs[1][...] if len(column_refs) > 1 else jnp.zeros_like(near)
    places = (0, cells, cells + 16, cells + 32, cells + 32 + width)
    values = (main_ref[...], jnp.where(even, far, near), jnp.where(even, near, far), top_ref[...], bottom_ref[...])
    for place, value in zip(places, values):
        rows_ref[place : place + value.shape[0], :] = value
    shape = ((width + 2) * 16, rows_ref.shape[0])
    target = lax.broadcasted_iota(jnp.int32, shape, 0)
    source = lax.broadcasted_iota(jnp.int32, shape, 1)
    column, row = lax.shift_right_logical(target, 4), target & 15
    want = (row - 1) * width + (column - 1)
    want = jnp.where(row == 0, places[3] + column - 1, want)
    want = jnp.where(row == ROWS + 1, places[4] + column - 1, want)
    want = jnp.where(column == 0, places[1] + row, want)
    want = jnp.where(column == width + 1, places[2] + row, want)
    want = jnp.where(row > ROWS + 1, -1, want)
    pick = jnp.where(source == want, 1.0, 0.0).astype(BF16)
    picked = jnp.dot(pick, rows_ref[...], preferred_element_type=F32).astype(BF16)
    grad = jnp.dot(picked, mix_ref[...], preferred_element_type=F32)
    grad_ref[...] = grad.reshape(width + 2, 16, hidden)


TAPS = [(a, b) for a in range(3) for b in range(3)]


def middle_kernel(tiles, lane, grad_ref, depth_ref, *refs):
    term_refs, (act_grad_ref, hidden_ref, act, inner) = refs[:tiles], refs[tiles:]
    width = grad_ref.shape[0] - 2
    cols = lax.axis_size("col")
    pairs = sent_pairs(width, cols)
    main = ROWS * pairs
    before_block = jnp.where(lax.axis_index("col") == 0, 2, 0) if cols == 2 else 0
    chunks = [
        (n, slice(n * LANES, (n + 1) * LANES), slice(lane + n * LANES, lane + (n + 1) * LANES))
        for n in range(act.shape[0])
    ]
    for n, here, _ in chunks:
        total = tree_sum([ref[:, here].astype(F32) for ref in term_refs]).astype(BF16).astype(F32)
        for p in range(pairs):
            for half in range(2):
                column = before_block + 2 * p + half
                start = half * main + ROWS * p
                act[n, column, 2 : 2 + ROWS, :] = total[start : start + ROWS]
                start = 2 * main + ROWS * p + 4 * half
                act[n, column, 0:2, :] = total[start : start + 2]
                act[n, column, 2 + ROWS : 4 + ROWS, :] = total[start + 2 : start + 4]
        if cols == 2:
            for half in range(2):
                act[n, lax.rem(before_block + width + 2, width + 4) + half] = jnp.zeros(act.shape[2:], F32)

    def forward(column, carry):
        for n, here, whole in chunks:
            terms = [
                depth_ref[3 * a + b : 3 * a + b + 1, whole] * act[n, column + b, a : a + ROWS + 2, :] for a, b in TAPS
            ]
            before = tree_sum(terms)
            sig = 1.0 / (1.0 + jnp.exp(-before))
            slope = sig * (1.0 + before * (1.0 - sig))
            grad = grad_ref[column, 0 : ROWS + 2, whole] * slope
            inner[n, column, 0 : ROWS + 2, :] = grad.astype(BF16).astype(F32)
            hidden_ref[column, :, here] = (before * sig)[1 : ROWS + 1]
        return carry

    lax.fori_loop(0, width + 2, forward, 0)

    def backward(column, carry):
        place = lax.shift_right_logical(column, 1) + (column & 1) * (width // 2)
        for n, here, whole in chunks:
            terms = [
                depth_ref[3 * a + b : 3 * a + b + 1, whole] * inner[n, column + 2 - b, 2 - a : 2 - a + ROWS, :]
                for a, b in TAPS
            ]
            act_grad_ref[place, :, here] = tree_sum(terms).astype(BF16)
        return carry

    lax.fori_loop(0, width, backward, 0)


def finish_kernel(parts, upstream_ref, mix_ref, *refs):
    hidden_refs, acts, inners = (refs[parts * i : parts * (i + 1)] for i in range(3))
    adjusted_ref, keep_ref, send_ref, held = refs[3 * parts :]
    own, columns = acts[0].shape[:2]
    chunks = own * parts
    width = columns - 4
    cells, hidden = upstream_ref.shape
    target = lax.broadcasted_iota(jnp.int32, (cells, cells), 0)
    source = lax.broadcasted_iota(jnp.int32, (cells, cells), 1)
    pick = (source & (ROWS - 1)) * width + lax.shift_right_logical(source, 3) == target
    pick = jnp.where(pick, 1.0, 0.0).astype(BF16)
    by_column = jnp.concatenate(
        [ref[1 : width + 1].reshape(cells, -1).astype(BF16) for ref in hidden_refs], axis=1
    )
    value = jnp.dot(pick, by_column, preferred_element_type=F32).astype(BF16)
    adjusted_ref[...] = lax.dot_general(
        value, mix_ref[...], (((1,), (1,)), ((), ())), preferred_element_type=F32
    ).astype(BF16)
    held[...] = lax.dot_general(
        upstream_ref[...], value, (((0,), (0,)), ((), ())), preferred_element_type=F32
    ).astype(BF16)

    def add(column, sums):
        new = []
        for n in range(chunks):
            act, grad = acts[n // own], inners[n // own][n % own, column + 1, 1 : 1 + ROWS, :]
            for t, (a, b) in enumerate(TAPS):
                new.append(sums[n * 9 + t] + act[n % own, column + 1 + b, 1 + a : 1 + a + ROWS, :] * grad)
        return tuple(new)

    zero = jnp.zeros((ROWS, LANES), F32)
    sums = lax.fori_loop(0, width, add, (zero,) * (9 * chunks))
    rows = []
    for n in range(chunks):
        taps = [jnp.sum(sums[n * 9 + t], axis=0, keepdims=True) for t in range(9)]
        rows.append(jnp.concatenate(taps + [jnp.zeros((7, LANES), F32)], axis=0))
    depth = jnp.concatenate(rows, axis=1).astype(BF16)
    rep = lax.axis_index("rep")
    block = hidden // (lax.axis_size("tile") * lax.axis_size("col") * lax.axis_size("rep"))
    for ref, which in ((keep_ref, rep), (send_ref, 1 - rep)):
        for g in range((keep_ref.shape[0] - 16) // block):
            start = pl.multiple_of(2 * g * block + which * block, 16)
            ref[g * block : (g + 1) * block, :] = held[pl.ds(start, block), :]
        ref[keep_ref.shape[0] - 16 :, :] = depth


def spread_kernel(axis, block, count, *refs):
    in_refs, out_refs, held = refs[:count], refs[count:-1], refs[-1]
    held[...] = tree_sum([ref[...].astype(F32) for ref in in_refs]).astype(BF16)
    rows = out_refs[0].shape[0] - 16
    size = len(out_refs)
    for step, out in enumerate(out_refs):
        part = lax.bitwise_xor(lax.axis_index(axis), step)
        for g in range(rows // block):
            start = pl.multiple_of(g * size * block + part * block, 16)
            out[g * block : (g + 1) * block, :] = held[pl.ds(start, block), :]
        out[rows:, :] = held[held.shape[0] - 16 :, :]


def total_kernel(count, *refs):
    in_refs, (mix_ref, depth_ref) = refs[:count], refs[count:]
    total = tree_sum([ref[...].astype(F32) for ref in in_refs])
    rows = mix_ref.shape[0]
    mix_ref[...] = total[:rows]
    depth_ref[...] = total[rows : rows + depth_ref.shape[0]]


def corner_kernel(ends, sides, *refs):
    row_refs, edge_refs, (top_ref, bottom_ref), out_refs = (
        refs[:ends],
        refs[ends : ends + sides],
        refs[ends + sides : ends + sides + 2],
        refs[ends + sides + 2 :],
    )
    even = lax.rem(lax.axis_index("tile"), 2) == 0
    near = row_refs[0][...].astype(F32)
    far = row_refs[1][...].astype(F32) if ends > 1 else jnp.zeros_like(near)
    top, bottom = jnp.where(even, far, near), jnp.where(even, near, far)
    top_ref[...] = top.astype(BF16)
    bottom_ref[...] = bottom.astype(BF16)
    last = lax.rem(lax.axis_index("col"), 2) == 0
    for i, (edge, out) in enumerate(zip(edge_refs, out_refs)):
        pick = last if i == 0 else ~last
        ends_of = [jnp.where(pick, row[-1:], row[:1]) for row in (top, bottom)]
        blank = jnp.zeros((16 - ROWS - 2, top.shape[1]), F32)
        out[...] = jnp.concatenate([ends_of[0], edge[...].astype(F32), ends_of[1], blank], axis=0).astype(BF16)


def by_band(grad_refs, whole):
    cells = grad_refs[0].shape[0]
    for step, ref in enumerate(grad_refs):
        start = pl.multiple_of(lax.bitwise_xor(lax.axis_index("tile"), step) * cells, 16)
        whole[pl.ds(start, cells), :] = ref[...]


def in_gradient_kernel(tiles, own_ref, *refs):
    grad_refs, (keep, send, whole, held) = refs[:tiles], refs[tiles:]
    by_band(grad_refs, whole)
    term = lax.dot_general(own_ref[...], whole[...], (((0,), (0,)), ((), ())), preferred_element_type=F32)
    half = keep.shape[0]
    rep = lax.axis_index("rep")
    held[...] = term[: 2 * half].astype(BF16)
    keep[...] = held[pl.ds(pl.multiple_of(rep * half, 16), half), :]
    send[...] = held[pl.ds(pl.multiple_of((1 - rep) * half, 16), half), :]


def group_gradient_kernel(tiles, parts, own_ref, weight_ref, patch_ref, *refs):
    whole_refs, grad_refs = refs[: parts - 1], refs[parts - 1 : parts - 1 + tiles]
    group_keep, group_send, last, group_term = refs[parts - 1 + tiles :]
    slots, lanes = patch_ref.shape[0], 6 * LANES
    channels = LANES // 2
    by_band(grad_refs, last)
    rows = last[...]
    wide = rows.shape[1]
    cells = rows.shape[0] // tiles
    rep = lax.axis_index("rep")
    term = lax.dot_general(own_ref[...], rows, (((0,), (0,)), ((), ())), preferred_element_type=F32)
    group_term[:, :wide] = term[: slots * channels].astype(BF16)
    feature_grad = None
    for i, ref in enumerate((*whole_refs, last)):
        term = lax.dot_general(
            ref[...],
            weight_ref[:, i * wide : (i + 1) * wide],
            (((1,), (1,)), ((), ())),
            preferred_element_type=F32,
        )
        feature_grad = term if feature_grad is None else feature_grad + term
    feature_grad = feature_grad.astype(BF16).astype(F32)
    blank = slots * channels % LANES
    if blank:
        feature_grad = jnp.concatenate(
            [feature_grad, jnp.zeros((feature_grad.shape[0], LANES - blank), F32)], axis=1
        )
    part = cells // 2

    def halves(value):
        return [
            jnp.concatenate(
                [value[cells * j + part * h : cells * j + part * (h + 1)] for j in range(tiles)], axis=0
            )
            for h in range(2)
        ]

    for slot in range(0, slots, 2):
        tile = feature_grad[:, slot * channels : slot * channels + LANES]
        both = interleave(*halves(tile))
        for k in range(slot, min(slot + 2, slots)):
            inner = (both[k - slot] * patch_ref[k, :, lanes:].astype(F32)).astype(BF16)
            term = lax.dot_general(inner, patch_ref[k, :, :lanes], (((0,), (0,)), ((), ())), preferred_element_type=F32)
            quarter = lanes // 3
            use = 3 * channels
            low = jnp.concatenate([term[:channels, quarter * a : quarter * a + use] for a in range(3)], axis=1)
            high = jnp.concatenate(
                [term[channels:, quarter * a + channels : quarter * (a + 1)] for a in range(3)], axis=1
            )
            blank = jnp.zeros((channels, -9 * channels % LANES), F32)
            group_term[channels * k : channels * (k + 1), wide:] = jnp.concatenate(
                [low + high, blank], axis=1
            ).astype(BF16)
    half = group_keep.shape[0]
    group_keep[...] = group_term[pl.ds(pl.multiple_of(rep * half, 16), half), :]
    group_send[...] = group_term[pl.ds(pl.multiple_of((1 - rep) * half, 16), half), :]


def call(kernel, outs, operands, scratch=(), flops=1 << 24, specs=None):
    shapes = [jax.ShapeDtypeStruct(s, d) for s, d in outs]
    moved = sum(o.size * o.dtype.itemsize for o in list(operands) + shapes)
    held = sum(math.prod(r.shape) * 4 for r in scratch if len(r.shape) > 1)
    return pl.pallas_call(
        kernel,
        out_shape=shapes,
        in_specs=specs or [SMEM if jnp.issubdtype(o.dtype, jnp.integer) else VMEM for o in operands],
        out_specs=[VMEM] * len(shapes),
        scratch_shapes=list(scratch),
        cost_estimate=pl.CostEstimate(flops=flops, bytes_accessed=moved, transcendentals=0),
        compiler_params=pltpu.CompilerParams(vmem_limit_bytes=(8 << 20) + 2 * (moved + held)),
    )(*operands)


def program(
    forcing,
    member_kernel_weight,
    member_counts,
    mixing_input_weight,
    depth_weight,
    mix_weight,
    cotangent,
):
    channels = member_kernel_weight.shape[2]
    slots = forcing.shape[1]
    height = forcing.shape[2]
    width = forcing.shape[3] // channels
    hidden = mixing_input_weight.shape[1]
    tiles, cols, reps = (lax.axis_size(a) for a in ("tile", "col", "rep"))
    pairs = sent_pairs(width, cols)
    cells = ROWS * width
    assert height == ROWS * tiles and 2 * channels == LANES
    lane_tiles = -(-slots // 2)
    rows = hidden // (tiles * cols * reps)
    parts = 2
    wide = hidden // parts

    sides, ends = (1 if count == 2 else 2 for count in (cols, tiles))
    field, kernel, weight, upstream, *edges = call(
        functools.partial(prepare_kernel, (sides, ends)),
        [
            (forcing.shape[1:], BF16),
            ((slots, LANES, 6 * LANES), BF16),
            ((lane_tiles * LANES, hidden), BF16),
            (cotangent.shape[1:], BF16),
        ]
        + [((slots, height, 4 * channels), BF16)] * sides
        + [((ROWS, hidden), BF16)] * sides
        + [((width, hidden), BF16)] * ends,
        [
            pltpu.with_memory_space_constraint(x, pltpu.HBM)
            for x in (forcing[0], jnp.swapaxes(member_kernel_weight, 1, 2), mixing_input_weight, cotangent[0])
        ],
        [pltpu.VMEM((slots, channels, 9 * channels), BF16), pltpu.SemaphoreType.DMA((4,))],
        specs=[HBM] * 4,
    )
    halos = with_neighbours(edges[:sides], "col")
    rows_near = with_neighbours(edges[2 * sides :], "tile")
    sent = call(
        functools.partial(features_kernel, tiles, pairs, parts),
        [((3 * ROWS * pairs, wide), BF16)] * (tiles * parts),
        [member_counts, field, kernel, weight, *halos],
        [pltpu.VMEM((tiles, 3 * ROWS * pairs, lane_tiles * LANES), BF16)],
        flops=1 << 28,
    )
    terms = [
        [swap(term, "tile", step) if step else term for step, term in enumerate(sent[h * tiles : (h + 1) * tiles])]
        for h in range(parts)
    ]

    top, bottom, *columns = call(
        functools.partial(corner_kernel, ends, sides),
        [((width, hidden), BF16)] * 2 + [((16, hidden), BF16)] * sides,
        [*rows_near, *edges[sides : 2 * sides]],
    )
    columns = with_neighbours(columns, "col")
    flat_upstream = upstream.reshape(cells, hidden)
    (hidden_grad,) = call(
        upstream_kernel,
        [((width + 2, 16, hidden), F32)],
        [flat_upstream, top, bottom, mix_weight, *columns],
        [pltpu.VMEM((2 * LANES, hidden), BF16)],
        flops=1 << 28,
    )
    patch, own_features = call(
        backward_inputs_kernel,
        [
            ((slots, cells // 2 * tiles, 7 * LANES), BF16),
            ((cells * tiles, lane_tiles * LANES), BF16),
        ],
        [member_counts, field, kernel, *halos],
        flops=1 << 28,
    )

    middles, grads = [], []
    for h in range(parts):
        act_grad, *rest = call(
            functools.partial(middle_kernel, tiles, h * wide),
            [
                ((width, ROWS, wide), BF16),
                ((width + 2, ROWS, wide), F32),
                ((wide // LANES, width + 4, 16, LANES), F32),
                ((wide // LANES, width + 2, 16, LANES), F32),
            ],
            [hidden_grad, depth_weight, *terms[h]],
        )
        act_grad = act_grad.reshape(cells, wide)
        grads.append([swap(act_grad, "tile", step) if step else act_grad for step in range(tiles)])
        middles.append(rest)

    part = ((tiles * cols * rows + 16, hidden), BF16)
    adjusted, keep, send = call(
        functools.partial(finish_kernel, parts),
        [((cells, hidden), BF16), part, part],
        [flat_upstream, mix_weight, *(middles[h][i] for i in range(3) for h in range(parts))],
        [pltpu.VMEM((hidden, hidden), BF16)],
    )
    arrived = [keep, swap(send, "rep", 1)]
    blocks = tiles * cols
    for axis in ("col", "tile"):
        size = lax.axis_size(axis)
        blocks //= size
        dealt = call(
            functools.partial(spread_kernel, axis, rows, len(arrived)),
            [((blocks * rows + 16, hidden), BF16)] * size,
            arrived,
            [pltpu.VMEM(arrived[0].shape, BF16)],
        )
        arrived = [swap(dealt[step], axis, step) if step else dealt[0] for step in range(size)]
    mix_grad, depth_grad = call(
        functools.partial(total_kernel, tiles), [((rows, hidden), F32), ((9, hidden), F32)], arrived
    )

    half = slots * channels // 2
    joined, wholes = [], []
    for h in range(parts - 1):
        keep, send, whole = call(
            functools.partial(in_gradient_kernel, tiles),
            [((half, wide), BF16), ((half, wide), BF16), ((cells * tiles, wide), BF16)],
            [own_features, *grads[h]],
            [pltpu.VMEM((2 * half, wide), BF16)],
        )
        wholes.append(whole)
        joined += full_sum(keep, send)
    lanes = wide + 9 * channels + -9 * channels % LANES
    keep, send = call(
        functools.partial(group_gradient_kernel, tiles, parts),
        [((half, lanes), BF16), ((half, lanes), BF16)],
        [own_features, mixing_input_weight, patch, *wholes, *grads[-1]],
        [pltpu.VMEM((cells * tiles, wide), BF16), pltpu.VMEM((2 * half, lanes), BF16)],
        flops=1 << 28,
    )
    joined += full_sum(keep, send)
    in_grad, group_grad = call(
        functools.partial(join_kernel, parts), [((2 * half, hidden), F32), ((2 * half, 9 * channels), F32)], joined
    )
    group_grad = jnp.swapaxes(group_grad.reshape(slots, channels, -1), 1, 2)
    return (adjusted.reshape(cotangent.shape), mix_grad, depth_grad, in_grad, group_grad)


def solution(mesh):
    in_specs = (
        P(("groups", "rep"), "tile", None, "col"),
        P("tile", None, None),
        P("tile"),
        P("tile", None),
        P(),
        P(),
        P(("groups", "rep"), "tile", "col", None),
    )
    out_specs = (
        P(("groups", "rep"), "tile", "col", None),
        P(("groups", "tile", "col", "rep"), None),
        P("groups", None),
        P(("groups", "tile"), None),
        P(("groups", "tile"), None, None),
    )
    return jax.shard_map(program, mesh=mesh, in_specs=in_specs, out_specs=out_specs, check_vma=False)
```

```python
import functools
import math

import jax
import jax.numpy as jnp
from jax import lax
from jax.experimental import pallas as pl
from jax.experimental.pallas import tpu as pltpu
from jax.sharding import PartitionSpec as P


F32 = jnp.float32
BF16 = jnp.bfloat16
LANES = 128
ROWS = 8
VMEM = pl.BlockSpec(memory_space=pltpu.VMEM)
SMEM = pl.BlockSpec(memory_space=pltpu.SMEM)
HBM = pl.BlockSpec(memory_space=pltpu.HBM)


def swap(value, axis, step):
    return lax.ppermute(value, axis, [(i, i ^ step) for i in range(lax.axis_size(axis))])


def with_neighbours(values, axis):
    count = lax.axis_size(axis)
    received = []
    for first, value in enumerate(values):
        pairs = [(i, i + 1) for i in range(first, count - 1, 2)]
        received.append(lax.ppermute(value, axis, pairs + [(b, a) for a, b in pairs]))
    return received


def tree_sum(terms):
    while len(terms) > 1:
        terms = [a + b for a, b in zip(terms[::2], terms[1::2])] + terms[len(terms) & ~1 :]
    return terms[0]


def full_sum(keep, send):
    def add(first, second):
        return (first.astype(F32) + second.astype(F32)).astype(BF16)

    total = add(keep, swap(send, "rep", 1))
    step = 1
    while step < lax.axis_size("col"):
        total = add(total, swap(total, "col", step))
        step *= 2
    return total, swap(total, "rep", 1)


def join_kernel(parts, *refs):
    in_refs, mix_refs, (in_out, group_out, mix_out, depth_out) = refs[: 2 * parts], refs[2 * parts : -4], refs[-4:]
    total = tree_sum([ref[...].astype(F32) for ref in mix_refs])
    mix_out[...] = total[: mix_out.shape[0]]
    depth_out[...] = total[mix_out.shape[0] : mix_out.shape[0] + depth_out.shape[0]]
    rows = in_refs[0].shape[0]
    rep = lax.axis_index("rep")
    for i in range(parts):
        for ref, which in ((in_refs[2 * i], rep), (in_refs[2 * i + 1], 1 - rep)):
            here = pl.ds(pl.multiple_of(which * rows, 16), rows)
            wide = in_refs[0].shape[1] if i < parts - 1 else in_out.shape[1] - i * in_refs[0].shape[1]
            at = in_out.shape[1] - wide if i == parts - 1 else i * wide
            in_out[here, at : at + wide] = ref[:, :wide].astype(F32)
            if i == parts - 1:
                group_out[here, :] = ref[:, wide : wide + group_out.shape[1]].astype(F32)


def silu_slope(value):
    sig = 1.0 / (1.0 + jnp.exp(-value))
    return sig * (1.0 + value * (1.0 - sig))


def lane_below(shape, bound):
    return lax.broadcasted_iota(jnp.int32, shape, len(shape) - 1) < bound


def interleave(first, second):
    half = LANES // 2
    low = lane_below(first.shape, half)
    axis = first.ndim - 1
    return (
        jnp.where(low, first, pltpu.roll(second, half, axis)),
        jnp.where(low, pltpu.roll(first, half, axis), second),
    )


def window_rows(field_ref, halo_refs, slot, inner):
    even = lax.rem(lax.axis_index("col"), 2) == 0
    near = halo_refs[0][slot].astype(F32)
    far = halo_refs[1][slot].astype(F32) if len(halo_refs) > 1 else jnp.zeros_like(near)
    left, right = jnp.where(even, far, near), jnp.where(even, near, far)
    whole = jnp.concatenate([left, field_ref[slot].astype(F32), right], axis=1)
    half = LANES // 2
    tiles = [whole[:, i : i + LANES] for i in range(0, whole.shape[1], LANES)]
    low = lane_below(tiles[0].shape, half)
    tiles = [pltpu.roll(t, half, 1) for t in tiles]
    tiles = [jnp.where(low, a, b) for a, b in zip(tiles, tiles[1:])]
    if inner:
        tiles = tiles[1:-1]
    elif len(halo_refs) == 1:
        tiles = [jnp.where(even, b, a) for a, b in zip(tiles, tiles[1:])]
    middle = jnp.concatenate(tiles, axis=1)
    height = middle.shape[0]
    row = lax.broadcasted_iota(jnp.int32, middle.shape, 0)
    above = jnp.where(row == 0, 0.0, pltpu.roll(middle, 1, 0))
    below = jnp.where(row == height - 1, 0.0, pltpu.roll(middle, height - 1, 0))
    return above, middle, below


def pair_weight(kernel_ref, slot):
    weight = kernel_ref[slot].astype(F32)
    span = weight.shape[1] // 3
    parts = [weight[:, a * span : (a + 1) * span] for a in range(3)]
    blank = jnp.zeros((weight.shape[0], LANES // 2), F32)
    first = jnp.concatenate([x for part in parts for x in (part, blank)], axis=1)
    second = jnp.concatenate([x for part in parts for x in (blank, part)], axis=1)
    return jnp.concatenate([first, second], axis=0).astype(BF16)


def prepare_kernel(edges_out, field, kernel, weight, upstream, *refs):
    field_ref, pair_ref, weight_ref, upstream_ref = refs[:4]
    field_edges, refs = refs[4 : 4 + edges_out[0]], refs[4 + edges_out[0] :]
    upstream_edges, row_edges = refs[: edges_out[0]], refs[edges_out[0] : -2]
    kernel_ref, sems = refs[-2:]
    depth = weight.shape[0]
    copies = [
        pltpu.make_async_copy(source, target, sems.at[i])
        for i, (source, target) in enumerate(
            (
                (field, field_ref),
                (upstream, upstream_ref),
                (kernel, kernel_ref),
                (weight, weight_ref.at[pl.ds(0, depth), :]),
            )
        )
    ]
    for copy in copies:
        copy.start()
    if weight_ref.shape[0] > depth:
        weight_ref[depth:, :] = jnp.zeros((weight_ref.shape[0] - depth, weight_ref.shape[1]), BF16)
    even = lax.rem(lax.axis_index("col"), 2) == 0
    reach = field_edges[0].shape[2]
    copies[0].wait()
    low, high = field_ref[:, :, :reach], field_ref[:, :, field_ref.shape[2] - reach :]
    for i, ref in enumerate(field_edges):
        ref[...] = jnp.where(even, low, high) if i else jnp.where(even, high, low)
    copies[1].wait()
    cells = upstream_ref[...].astype(F32)
    low, high = cells[:, 0, :], cells[:, cells.shape[1] - 1, :]
    for i, ref in enumerate(upstream_edges):
        ref[...] = (jnp.where(even, low, high) if i else jnp.where(even, high, low)).astype(BF16)
    even = lax.rem(lax.axis_index("tile"), 2) == 0
    low, high = upstream_ref[0], upstream_ref[upstream_ref.shape[0] - 1]
    for i, ref in enumerate(row_edges):
        ref[...] = jnp.where(even, low, high) if i else jnp.where(even, high, low)
    copies[2].wait()
    for slot in range(kernel_ref.shape[0]):
        pair_ref[slot] = pair_weight(kernel_ref, slot)
    copies[3].wait()


def gate_of(shifted, weight):
    shifted = [s.astype(BF16) for s in shifted]
    pairs = shifted[0].shape[1] // LANES - 1
    lhs = jnp.concatenate(
        [
            jnp.concatenate([s[:, p * LANES : (p + 2) * LANES] for s in shifted], axis=1)
            for p in range(pairs)
        ],
        axis=0,
    )
    gate = lax.dot_general(lhs, weight, (((1,), (1,)), ((), ())), preferred_element_type=F32)
    return gate.reshape(pairs, -1, LANES)


def sent_pairs(width, cols):
    return width // 2 + (1 if cols == 2 else 2)


def features_kernel(tiles, pairs, parts, count_ref, field_ref, kernel_ref, weight_ref, *refs):
    outs = tiles * parts
    halo_refs, out_refs, store = refs[: -outs - 1], refs[-outs - 1 : -1], refs[-1]
    slots, height, _ = field_ref.shape
    main = ROWS * pairs
    col = lax.axis_index("col")

    def values(slot):
        gate = gate_of(window_rows(field_ref, halo_refs, slot, False), kernel_ref[slot])
        value = gate / (1.0 + jnp.exp(-gate))
        live = slot < count_ref[0]
        if len(halo_refs) == 1:
            return jnp.where(live, value, 0.0)
        first = jnp.where(live & (col > 0), value[:1], 0.0)
        last = jnp.where(live & (col < lax.axis_size("col") - 1), value[-1:], 0.0)
        return jnp.concatenate([first, jnp.where(live, value[1:-1], 0.0), last], axis=0)

    def put(both, lane_tile):
        here = slice(lane_tile * LANES, (lane_tile + 1) * LANES)
        bands = [[v[:, ROWS * j : ROWS * (j + 1)] for j in range(height // ROWS)] for v in both]
        none = jnp.zeros_like(bands[0][0])
        sub = lax.broadcasted_iota(jnp.int32, none.shape, 1)
        for j in range(height // ROWS):
            halo = []
            for half in range(2):
                rows = bands[half][j].reshape(main, LANES)
                store[j, half * main : (half + 1) * main, here] = rows.astype(BF16)
                above = bands[half][j - 1] if j else none
                below = bands[half][j + 1] if ROWS * (j + 1) < height else none
                halo.append(pltpu.roll(jnp.where(sub >= 4, above, below), 2 + 4 * half, 1))
            store[j, 2 * main :, here] = jnp.where(sub < 4, *halo).reshape(main, LANES).astype(BF16)

    for slot in range(0, slots - 1, 2):
        put(interleave(values(slot), values(slot + 1)), slot // 2)
    if slots % 2:
        last = values(slots - 1)
        put(interleave(last, jnp.zeros_like(last)), slots // 2)
    for step in range(tiles):
        band = lax.bitwise_xor(lax.axis_index("tile"), step)
        term = jnp.dot(store[band], weight_ref[...], preferred_element_type=F32).astype(BF16)
        for part in range(parts):
            out = out_refs[part * tiles + step]
            out[...] = term[:, part * out.shape[1] : (part + 1) * out.shape[1]]


def backward_inputs_kernel(count_ref, field_ref, kernel_ref, *refs):
    halo_refs, (patch_ref, own_ref) = refs[:-2], refs[-2:]
    slots, height, lanes = field_ref.shape
    pairs = lanes // LANES
    bands = height // ROWS

    def by_band(value):
        return jnp.concatenate([value[:, ROWS * j : ROWS * (j + 1)] for j in range(bands)], axis=0)

    def values(slot):
        shifted = window_rows(field_ref, halo_refs, slot, True)
        gate = gate_of(shifted, kernel_ref[slot])
        live = slot < count_ref[0]
        slope = by_band(jnp.where(live, silu_slope(gate), 0.0))
        patch_ref[slot, :, 6 * LANES :] = slope.reshape(-1, LANES).astype(BF16)
        for a, s in enumerate(shifted):
            patch = jnp.concatenate(
                [
                    s[ROWS * j : ROWS * (j + 1), p * LANES : (p + 2) * LANES]
                    for j in range(bands)
                    for p in range(pairs)
                ],
                axis=0,
            )
            patch_ref[slot, :, 2 * a * LANES : 2 * (a + 1) * LANES] = patch.astype(BF16)
        return jnp.where(live, gate / (1.0 + jnp.exp(-gate)), 0.0)

    def put(even, odd, lane_tile):
        span = ROWS * pairs
        for j in range(bands):
            for half, value in enumerate((even, odd)):
                rows = value[:, ROWS * j : ROWS * (j + 1)].reshape(span, LANES)
                own_ref[
                    (2 * j + half) * span : (2 * j + half + 1) * span,
                    lane_tile * LANES : (lane_tile + 1) * LANES,
                ] = rows.astype(BF16)

    for slot in range(0, slots - 1, 2):
        put(*interleave(values(slot), values(slot + 1)), slot // 2)
    if slots % 2:
        last = values(slots - 1)
        put(*interleave(last, jnp.zeros_like(last)), slots // 2)


def upstream_kernel(main_ref, top_ref, bottom_ref, mix_ref, *refs):
    column_refs, (grad_ref, rows_ref) = refs[:-2], refs[-2:]
    width = grad_ref.shape[0] - 2
    cells, hidden = main_ref.shape
    rows_ref[...] = jnp.zeros_like(rows_ref)
    even = lax.rem(lax.axis_index("col"), 2) == 0
    near = column_refs[0][...]
    far = column_refs[1][...] if len(column_refs) > 1 else jnp.zeros_like(near)
    places = (0, cells, cells + 16, cells + 32, cells + 32 + width)
    values = (main_ref[...], jnp.where(even, far, near), jnp.where(even, near, far), top_ref[...], bottom_ref[...])
    for place, value in zip(places, values):
        rows_ref[place : place + value.shape[0], :] = value
    shape = ((width + 2) * 16, rows_ref.shape[0])
    target = lax.broadcasted_iota(jnp.int32, shape, 0)
    source = lax.broadcasted_iota(jnp.int32, shape, 1)
    column, row = lax.shift_right_logical(target, 4), target & 15
    want = (row - 1) * width + (column - 1)
    want = jnp.where(row == 0, places[3] + column - 1, want)
    want = jnp.where(row == ROWS + 1, places[4] + column - 1, want)
    want = jnp.where(column == 0, places[1] + row, want)
    want = jnp.where(column == width + 1, places[2] + row, want)
    want = jnp.where(row > ROWS + 1, -1, want)
    pick = jnp.where(source == want, 1.0, 0.0).astype(BF16)
    picked = jnp.dot(pick, rows_ref[...], preferred_element_type=F32).astype(BF16)
    grad = jnp.dot(picked, mix_ref[...], preferred_element_type=F32)
    grad_ref[...] = grad.reshape(width + 2, 16, hidden)


TAPS = [(a, b) for a in range(3) for b in range(3)]


def by_groups(count, most, step):
    group = max(g for g in range(1, most + 1) if count % g == 0)

    def body(i, carry):
        for j in range(group):
            step(i * group + j)
        return carry

    lax.fori_loop(0, count // group, body, 0)


def middle_kernel(tiles, lane, grad_ref, depth_ref, *refs):
    term_refs, (act_grad_ref, hidden_ref, act, inner) = refs[:tiles], refs[tiles:]
    width = grad_ref.shape[0] - 2
    cols = lax.axis_size("col")
    pairs = sent_pairs(width, cols)
    main = ROWS * pairs
    before_block = jnp.where(lax.axis_index("col") == 0, 2, 0) if cols == 2 else 0
    chunks = [
        (n, slice(n * LANES, (n + 1) * LANES), slice(lane + n * LANES, lane + (n + 1) * LANES))
        for n in range(act.shape[0])
    ]
    for n, here, _ in chunks:
        total = tree_sum([ref[:, here].astype(F32) for ref in term_refs]).astype(BF16).astype(F32)
        for p in range(pairs):
            for half in range(2):
                column = before_block + 2 * p + half
                start = half * main + ROWS * p
                act[n, column, 2 : 2 + ROWS, :] = total[start : start + ROWS]
                start = 2 * main + ROWS * p + 4 * half
                act[n, column, 0:2, :] = total[start : start + 2]
                act[n, column, 2 + ROWS : 4 + ROWS, :] = total[start + 2 : start + 4]
        if cols == 2:
            for half in range(2):
                act[n, lax.rem(before_block + width + 2, width + 4) + half] = jnp.zeros(act.shape[2:], F32)

    def forward(column):
        for n, here, whole in chunks:
            terms = [
                depth_ref[3 * a + b : 3 * a + b + 1, whole] * act[n, column + b, a : a + ROWS + 2, :] for a, b in TAPS
            ]
            before = tree_sum(terms)
            sig = 1.0 / (1.0 + jnp.exp(-before))
            slope = sig * (1.0 + before * (1.0 - sig))
            grad = grad_ref[column, 0 : ROWS + 2, whole] * slope
            inner[n, column, 0 : ROWS + 2, :] = grad.astype(BF16).astype(F32)
            hidden_ref[column, :, here] = (before * sig)[1 : ROWS + 1]

    by_groups(width + 2, 3, forward)

    def backward(column):
        place = lax.shift_right_logical(column, 1) + (column & 1) * (width // 2)
        for n, here, whole in chunks:
            terms = [
                depth_ref[3 * a + b : 3 * a + b + 1, whole] * inner[n, column + 2 - b, 2 - a : 2 - a + ROWS, :]
                for a, b in TAPS
            ]
            act_grad_ref[place, :, here] = tree_sum(terms).astype(BF16)

    by_groups(width, 4, backward)


def finish_kernel(parts, upstream_ref, mix_ref, *refs):
    hidden_refs, acts, inners = (refs[parts * i : parts * (i + 1)] for i in range(3))
    adjusted_ref, keep_ref, send_ref, held = refs[3 * parts :]
    own, columns = acts[0].shape[:2]
    chunks = own * parts
    width = columns - 4
    cells, hidden = upstream_ref.shape
    target = lax.broadcasted_iota(jnp.int32, (cells, cells), 0)
    source = lax.broadcasted_iota(jnp.int32, (cells, cells), 1)
    pick = (source & (ROWS - 1)) * width + lax.shift_right_logical(source, 3) == target
    pick = jnp.where(pick, 1.0, 0.0).astype(BF16)
    by_column = jnp.concatenate(
        [ref[1 : width + 1].reshape(cells, -1).astype(BF16) for ref in hidden_refs], axis=1
    )
    value = jnp.dot(pick, by_column, preferred_element_type=F32).astype(BF16)
    adjusted_ref[...] = lax.dot_general(
        value, mix_ref[...], (((1,), (1,)), ((), ())), preferred_element_type=F32
    ).astype(BF16)
    held[...] = lax.dot_general(
        upstream_ref[...], value, (((0,), (0,)), ((), ())), preferred_element_type=F32
    ).astype(BF16)

    def add(column, sums):
        new = []
        for n in range(chunks):
            act, grad = acts[n // own], inners[n // own][n % own, column + 1, 1 : 1 + ROWS, :]
            for t, (a, b) in enumerate(TAPS):
                new.append(sums[n * 9 + t] + act[n % own, column + 1 + b, 1 + a : 1 + a + ROWS, :] * grad)
        return tuple(new)

    zero = jnp.zeros((ROWS, LANES), F32)
    sums = lax.fori_loop(0, width, add, (zero,) * (9 * chunks))
    rows = []
    for n in range(chunks):
        taps = [jnp.sum(sums[n * 9 + t], axis=0, keepdims=True) for t in range(9)]
        rows.append(jnp.concatenate(taps + [jnp.zeros((7, LANES), F32)], axis=0))
    depth = jnp.concatenate(rows, axis=1).astype(BF16)
    rep = lax.axis_index("rep")
    block = hidden // (lax.axis_size("tile") * lax.axis_size("col") * lax.axis_size("rep"))
    for ref, which in ((keep_ref, rep), (send_ref, 1 - rep)):
        for g in range((keep_ref.shape[0] - 16) // block):
            start = pl.multiple_of(2 * g * block + which * block, 16)
            ref[g * block : (g + 1) * block, :] = held[pl.ds(start, block), :]
        ref[keep_ref.shape[0] - 16 :, :] = depth


def spread_kernel(axis, block, count, *refs):
    in_refs, out_refs, held = refs[:count], refs[count:-1], refs[-1]
    held[...] = tree_sum([ref[...].astype(F32) for ref in in_refs]).astype(BF16)
    rows = out_refs[0].shape[0] - 16
    size = len(out_refs)
    for step, out in enumerate(out_refs):
        part = lax.bitwise_xor(lax.axis_index(axis), step)
        for g in range(rows // block):
            start = pl.multiple_of(g * size * block + part * block, 16)
            out[g * block : (g + 1) * block, :] = held[pl.ds(start, block), :]
        out[rows:, :] = held[held.shape[0] - 16 :, :]


def corner_kernel(ends, sides, *refs):
    row_refs, edge_refs, (top_ref, bottom_ref), out_refs = (
        refs[:ends],
        refs[ends : ends + sides],
        refs[ends + sides : ends + sides + 2],
        refs[ends + sides + 2 :],
    )
    even = lax.rem(lax.axis_index("tile"), 2) == 0
    near = row_refs[0][...].astype(F32)
    far = row_refs[1][...].astype(F32) if ends > 1 else jnp.zeros_like(near)
    top, bottom = jnp.where(even, far, near), jnp.where(even, near, far)
    top_ref[...] = top.astype(BF16)
    bottom_ref[...] = bottom.astype(BF16)
    last = lax.rem(lax.axis_index("col"), 2) == 0
    for i, (edge, out) in enumerate(zip(edge_refs, out_refs)):
        pick = last if i == 0 else ~last
        ends_of = [jnp.where(pick, row[-1:], row[:1]) for row in (top, bottom)]
        blank = jnp.zeros((16 - ROWS - 2, top.shape[1]), F32)
        out[...] = jnp.concatenate([ends_of[0], edge[...].astype(F32), ends_of[1], blank], axis=0).astype(BF16)


def by_band(grad_refs, whole):
    cells = grad_refs[0].shape[0]
    for step, ref in enumerate(grad_refs):
        start = pl.multiple_of(lax.bitwise_xor(lax.axis_index("tile"), step) * cells, 16)
        whole[pl.ds(start, cells), :] = ref[...]


def in_gradient_kernel(tiles, own_ref, *refs):
    grad_refs, (keep, send, whole, held) = refs[:tiles], refs[tiles:]
    by_band(grad_refs, whole)
    term = lax.dot_general(own_ref[...], whole[...], (((0,), (0,)), ((), ())), preferred_element_type=F32)
    half = keep.shape[0]
    rep = lax.axis_index("rep")
    held[...] = term[: 2 * half].astype(BF16)
    keep[...] = held[pl.ds(pl.multiple_of(rep * half, 16), half), :]
    send[...] = held[pl.ds(pl.multiple_of((1 - rep) * half, 16), half), :]


def group_gradient_kernel(tiles, parts, own_ref, weight_ref, patch_ref, *refs):
    whole_refs, grad_refs = refs[: parts - 1], refs[parts - 1 : parts - 1 + tiles]
    group_keep, group_send, last, group_term = refs[parts - 1 + tiles :]
    slots, lanes = patch_ref.shape[0], 6 * LANES
    channels = LANES // 2
    by_band(grad_refs, last)
    rows = last[...]
    wide = rows.shape[1]
    cells = rows.shape[0] // tiles
    rep = lax.axis_index("rep")
    term = lax.dot_general(own_ref[...], rows, (((0,), (0,)), ((), ())), preferred_element_type=F32)
    group_term[:, :wide] = term[: slots * channels].astype(BF16)
    feature_grad = None
    for i, ref in enumerate((*whole_refs, last)):
        term = lax.dot_general(
            ref[...],
            weight_ref[:, i * wide : (i + 1) * wide],
            (((1,), (1,)), ((), ())),
            preferred_element_type=F32,
        )
        feature_grad = term if feature_grad is None else feature_grad + term
    feature_grad = feature_grad.astype(BF16).astype(F32)
    blank = slots * channels % LANES
    if blank:
        feature_grad = jnp.concatenate(
            [feature_grad, jnp.zeros((feature_grad.shape[0], LANES - blank), F32)], axis=1
        )
    part = cells // 2

    def halves(value):
        return [
            jnp.concatenate(
                [value[cells * j + part * h : cells * j + part * (h + 1)] for j in range(tiles)], axis=0
            )
            for h in range(2)
        ]

    for slot in range(0, slots, 2):
        tile = feature_grad[:, slot * channels : slot * channels + LANES]
        both = interleave(*halves(tile))
        for k in range(slot, min(slot + 2, slots)):
            inner = (both[k - slot] * patch_ref[k, :, lanes:].astype(F32)).astype(BF16)
            term = lax.dot_general(inner, patch_ref[k, :, :lanes], (((0,), (0,)), ((), ())), preferred_element_type=F32)
            quarter = lanes // 3
            use = 3 * channels
            low = jnp.concatenate([term[:channels, quarter * a : quarter * a + use] for a in range(3)], axis=1)
            high = jnp.concatenate(
                [term[channels:, quarter * a + channels : quarter * (a + 1)] for a in range(3)], axis=1
            )
            blank = jnp.zeros((channels, -9 * channels % LANES), F32)
            group_term[channels * k : channels * (k + 1), wide:] = jnp.concatenate(
                [low + high, blank], axis=1
            ).astype(BF16)
    half = group_keep.shape[0]
    group_keep[...] = group_term[pl.ds(pl.multiple_of(rep * half, 16), half), :]
    group_send[...] = group_term[pl.ds(pl.multiple_of((1 - rep) * half, 16), half), :]


def call(kernel, outs, operands, scratch=(), flops=1 << 24, specs=None):
    shapes = [jax.ShapeDtypeStruct(s, d) for s, d in outs]
    moved = sum(o.size * o.dtype.itemsize for o in list(operands) + shapes)
    held = sum(math.prod(r.shape) * 4 for r in scratch if len(r.shape) > 1)
    return pl.pallas_call(
        kernel,
        out_shape=shapes,
        in_specs=specs or [SMEM if jnp.issubdtype(o.dtype, jnp.integer) else VMEM for o in operands],
        out_specs=[VMEM] * len(shapes),
        scratch_shapes=list(scratch),
        cost_estimate=pl.CostEstimate(flops=flops, bytes_accessed=moved, transcendentals=0),
        compiler_params=pltpu.CompilerParams(vmem_limit_bytes=(8 << 20) + 2 * (moved + held)),
    )(*operands)


def program(
    forcing,
    member_kernel_weight,
    member_counts,
    mixing_input_weight,
    depth_weight,
    mix_weight,
    cotangent,
):
    channels = member_kernel_weight.shape[2]
    slots = forcing.shape[1]
    height = forcing.shape[2]
    width = forcing.shape[3] // channels
    hidden = mixing_input_weight.shape[1]
    tiles, cols, reps = (lax.axis_size(a) for a in ("tile", "col", "rep"))
    pairs = sent_pairs(width, cols)
    cells = ROWS * width
    assert height == ROWS * tiles and 2 * channels == LANES
    lane_tiles = -(-slots // 2)
    rows = hidden // (tiles * cols * reps)
    parts = 2
    wide = hidden // parts

    sides, ends = (1 if count == 2 else 2 for count in (cols, tiles))
    field, kernel, weight, upstream, *edges = call(
        functools.partial(prepare_kernel, (sides, ends)),
        [
            (forcing.shape[1:], BF16),
            ((slots, LANES, 6 * LANES), BF16),
            ((lane_tiles * LANES, hidden), BF16),
            (cotangent.shape[1:], BF16),
        ]
        + [((slots, height, 4 * channels), BF16)] * sides
        + [((ROWS, hidden), BF16)] * sides
        + [((width, hidden), BF16)] * ends,
        [
            pltpu.with_memory_space_constraint(x, pltpu.HBM)
            for x in (forcing[0], jnp.swapaxes(member_kernel_weight, 1, 2), mixing_input_weight, cotangent[0])
        ],
        [pltpu.VMEM((slots, channels, 9 * channels), BF16), pltpu.SemaphoreType.DMA((4,))],
        specs=[HBM] * 4,
    )
    halos = with_neighbours(edges[:sides], "col")
    rows_near = with_neighbours(edges[2 * sides :], "tile")
    sent = call(
        functools.partial(features_kernel, tiles, pairs, parts),
        [((3 * ROWS * pairs, wide), BF16)] * (tiles * parts),
        [member_counts, field, kernel, weight, *halos],
        [pltpu.VMEM((tiles, 3 * ROWS * pairs, lane_tiles * LANES), BF16)],
        flops=1 << 28,
    )
    terms = [
        [swap(term, "tile", step) if step else term for step, term in enumerate(sent[h * tiles : (h + 1) * tiles])]
        for h in range(parts)
    ]

    top, bottom, *columns = call(
        functools.partial(corner_kernel, ends, sides),
        [((width, hidden), BF16)] * 2 + [((16, hidden), BF16)] * sides,
        [*rows_near, *edges[sides : 2 * sides]],
    )
    columns = with_neighbours(columns, "col")
    flat_upstream = upstream.reshape(cells, hidden)
    (hidden_grad,) = call(
        upstream_kernel,
        [((width + 2, 16, hidden), F32)],
        [flat_upstream, top, bottom, mix_weight, *columns],
        [pltpu.VMEM((2 * LANES, hidden), BF16)],
        flops=1 << 28,
    )
    patch, own_features = call(
        backward_inputs_kernel,
        [
            ((slots, cells // 2 * tiles, 7 * LANES), BF16),
            ((cells * tiles, lane_tiles * LANES), BF16),
        ],
        [member_counts, field, kernel, *halos],
        flops=1 << 28,
    )

    middles, grads = [], []
    for h in range(parts):
        act_grad, *rest = call(
            functools.partial(middle_kernel, tiles, h * wide),
            [
                ((width, ROWS, wide), BF16),
                ((width + 2, ROWS, wide), F32),
                ((wide // LANES, width + 4, 16, LANES), F32),
                ((wide // LANES, width + 2, 16, LANES), F32),
            ],
            [hidden_grad, depth_weight, *terms[h]],
        )
        act_grad = act_grad.reshape(cells, wide)
        grads.append([swap(act_grad, "tile", step) if step else act_grad for step in range(tiles)])
        middles.append(rest)

    part = ((tiles * cols * rows + 16, hidden), BF16)
    adjusted, keep, send = call(
        functools.partial(finish_kernel, parts),
        [((cells, hidden), BF16), part, part],
        [flat_upstream, mix_weight, *(middles[h][i] for i in range(3) for h in range(parts))],
        [pltpu.VMEM((hidden, hidden), BF16)],
    )
    arrived = [keep, swap(send, "rep", 1)]
    blocks = tiles * cols
    for axis in ("col", "tile"):
        size = lax.axis_size(axis)
        blocks //= size
        dealt = call(
            functools.partial(spread_kernel, axis, rows, len(arrived)),
            [((blocks * rows + 16, hidden), BF16)] * size,
            arrived,
            [pltpu.VMEM(arrived[0].shape, BF16)],
        )
        arrived = [swap(dealt[step], axis, step) if step else dealt[0] for step in range(size)]
    half = slots * channels // 2
    joined, wholes = [], []
    for h in range(parts - 1):
        keep, send, whole = call(
            functools.partial(in_gradient_kernel, tiles),
            [((half, wide), BF16), ((half, wide), BF16), ((cells * tiles, wide), BF16)],
            [own_features, *grads[h]],
            [pltpu.VMEM((2 * half, wide), BF16)],
        )
        wholes.append(whole)
        joined += full_sum(keep, send)
    lanes = wide + 9 * channels + -9 * channels % LANES
    keep, send = call(
        functools.partial(group_gradient_kernel, tiles, parts),
        [((half, lanes), BF16), ((half, lanes), BF16)],
        [own_features, mixing_input_weight, patch, *wholes, *grads[-1]],
        [pltpu.VMEM((cells * tiles, wide), BF16), pltpu.VMEM((2 * half, lanes), BF16)],
        flops=1 << 28,
    )
    joined += full_sum(keep, send)
    in_grad, group_grad, mix_grad, depth_grad = call(
        functools.partial(join_kernel, parts),
        [((2 * half, hidden), F32), ((2 * half, 9 * channels), F32), ((rows, hidden), F32), ((9, hidden), F32)],
        [*joined, *arrived],
    )
    group_grad = jnp.swapaxes(group_grad.reshape(slots, channels, -1), 1, 2)
    return (adjusted.reshape(cotangent.shape), mix_grad, depth_grad, in_grad, group_grad)


def solution(mesh):
    in_specs = (
        P(("groups", "rep"), "tile", None, "col"),
        P("tile", None, None),
        P("tile"),
        P("tile", None),
        P(),
        P(),
        P(("groups", "rep"), "tile", "col", None),
    )
    out_specs = (
        P(("groups", "rep"), "tile", "col", None),
        P(("groups", "tile", "col", "rep"), None),
        P("groups", None),
        P(("groups", "tile"), None),
        P(("groups", "tile"), None, None),
    )
    return jax.shard_map(program, mesh=mesh, in_specs=in_specs, out_specs=out_specs, check_vma=False)
```
